512 devices in a mesh: section: 16 (over x, y_lo, core), tensor: 32 (over y_hi, z).
Axes of the slice: x: 4, y: 8 (y_hi: 4, y_lo: 2; y = y_hi * 2 + y_lo), z: 8, core: 2. Of those that a mesh axis runs over, the one named last changes fastest.
Arguments:
- hidden: bfloat16 [16, 256, 8192], P('section', 'tensor'), may hold values from -60 to 60
- norm_gain: float32 [8192], replicated, may hold values from 0.1 to 1.9
- lengths: int32 [16], P('section'), may hold values from 64 to 256
- query_param: float32 [8192, 4096], P(('section', 'tensor')), may hold values from -1.3258252 to 1.3258252
- query_grad: float32 [8192, 4096], P(('section', 'tensor')), may hold values from -0.006 to 0.006
- query_moment: float32 [8192, 4096], P(('section', 'tensor')), may hold values from -0.006 to 0.006
- query_second: float32 [8192, 4096], P(('section', 'tensor')), may hold values from 1e-07 to 1e-05
- keyval_param: float32 [8192, 1024], P(('section', 'tensor')), may hold values from -0.06629126 to 0.06629126
- keyval_gradient: float32 [8192, 1024], P(('section', 'tensor')), may hold values from -0.006 to 0.006
- keyval_first_moment: float32 [8192, 1024], P(('section', 'tensor')), may hold values from -0.006 to 0.006
- keyval_second_moment: float32 [8192, 1024], P(('section', 'tensor')), may hold values from 1e-07 to 1e-05
- output_param: float32 [8192, 4096], P(('section', 'tensor')), may hold values from -0.25 to 0.25
- output_grad: float32 [8192, 4096], P(('section', 'tensor')), may hold values from -0.006 to 0.006
- output_moment: float32 [8192, 4096], P(('section', 'tensor')), may hold values from -0.006 to 0.006
- output_second: float32 [8192, 4096], P(('section', 'tensor')), may hold values from 1e-07 to 1e-05
Outputs:
- mixed: bfloat16 [16, 256, 8192], P('section', 'tensor')
The draws below stay inside these ranges and needn't reach their ends.
All inputs are finite; a program needn't handle non-finite values.
Results may differ from the reference program's by a relative error of at most 0.017.
Values may be sent and summed in bfloat16 or wider, within the bound.
No kernel may reach another device: no remote copies, remote signals or barrier semaphores. Data moves between devices by JAX's collectives and lax.ppermute only.
A program may use at most 64 MiB of HBM per device.

```python
import math
import jax
import jax.numpy as jnp
from jax import lax

MODEL_DIMENSION = 8192
QUERY_HEADS_LOCAL = 32
KEYVAL_HEADS = 4
HEAD_DIMENSION = 128
PROMPT_LENGTH = 256
PROMPTS = 16
N_TENSOR = 32


def joint_weights(key):
    base_key = jax.random.fold_in(key, 7)
    key_query, keyval_random_key = jax.random.split(base_key, 2)
    query_part = jnp.clip(jax.random.normal(key_query, (MODEL_DIMENSION, QUERY_HEADS_LOCAL * HEAD_DIMENSION), jnp.float32), -6.0, 6.0) * MODEL_DIMENSION ** (-0.5)
    keyval_piece_slice = jnp.clip(jax.random.normal(keyval_random_key, (MODEL_DIMENSION, 2 * KEYVAL_HEADS * HEAD_DIMENSION), jnp.float32), -6.0, 6.0) * MODEL_DIMENSION ** (-0.5)
    return (query_part, keyval_piece_slice)


def draw_query_param(key, part):
    return joint_weights(key)[0]


def draw_keyval_param(key, part):
    return joint_weights(key)[1]


def draw_hidden(key, part):
    key_rows, key_columns_part, key_normal = jax.random.split(jax.random.fold_in(key, 11), 3)
    row_scale = jnp.exp(jax.random.uniform(key_rows, (PROMPTS, PROMPT_LENGTH, 1), jnp.float32, -1.204, 1.098))
    col_scale = jnp.exp(jax.random.uniform(key_columns_part, (1, 1, MODEL_DIMENSION), jnp.float32, -1.204, 1.098))
    normal_part = jnp.clip(jax.random.normal(key_normal, (PROMPTS, PROMPT_LENGTH, MODEL_DIMENSION), jnp.float32), -4.0, 4.0)
    return (normal_part * row_scale * col_scale).astype(jnp.bfloat16)


def draw_lengths(key, part):
    key_values, key_index = jax.random.split(jax.random.fold_in(key, 3))
    values = jax.random.randint(key_values, (PROMPTS,), PROMPT_LENGTH // 4, PROMPT_LENGTH + 1)
    full_index = jax.random.randint(key_index, (), 0, PROMPTS)
    return jnp.where(jnp.arange(PROMPTS) == full_index, PROMPT_LENGTH, values).astype(jnp.int32)


def block_scale(stream_key, extent, cuts, smallest, high):
    def one(axis_at, blocks):
        draws = jax.random.uniform(jax.random.fold_in(jax.random.fold_in(stream_key, 6), axis_at), (blocks,), jnp.float32, smallest / len(cuts), high / len(cuts))
        return jnp.repeat(jnp.exp(draws), extent[axis_at] // blocks).reshape((-1,) + (1,) * (len(extent) - axis_at - 1))

    factor_of = one(*cuts[0])
    for cut in cuts[1:]:
        factor_of = factor_of * one(*cut)
    return factor_of


def noise(own_key, dims, scale, limit, cuts=(), kind=jnp.bfloat16):
    level = block_scale(own_key, dims, cuts, -0.22, 0.18) if cuts else 1.0
    array = jax.random.normal(own_key, dims, jnp.float32) * scale * level
    return jnp.minimum(jnp.maximum(array, -limit), limit).astype(kind)


def setup_inputs(seed: int = 0) -> dict:
    key_of = jax.random.split(jax.random.key(seed), 16)
    hidden = draw_hidden(jax.random.fold_in(key_of[15], 71), 0)
    norm_gain = jnp.clip(1.0 + 0.18 * jax.random.normal(key_of[1], (MODEL_DIMENSION,), jnp.float32), 0.1, 1.9)
    lengths = draw_lengths(jax.random.fold_in(key_of[15], 71), 0)
    query_param = draw_query_param(jax.random.fold_in(key_of[15], 71), 0)
    query_grad = noise(key_of[4], (MODEL_DIMENSION, QUERY_HEADS_LOCAL * HEAD_DIMENSION), 0.001, 0.006, ((0, 512),), jnp.float32)
    query_moment = noise(key_of[5], (MODEL_DIMENSION, QUERY_HEADS_LOCAL * HEAD_DIMENSION), 0.001, 0.006, ((0, 512),), jnp.float32)
    query_second = jnp.clip(jnp.exp(math.log(9.999999747378752e-06) - 4.6051701 * jax.random.uniform(key_of[6], (MODEL_DIMENSION, QUERY_HEADS_LOCAL * HEAD_DIMENSION), jnp.float32) ** block_scale(key_of[6], (MODEL_DIMENSION, QUERY_HEADS_LOCAL * HEAD_DIMENSION), ((0, 512),), -0.2, 0.2)), 1.0000000116860974e-07, 9.999999747378752e-06)
    keyval_param = draw_keyval_param(jax.random.fold_in(key_of[15], 71), 0)
    keyval_gradient = noise(key_of[8], (MODEL_DIMENSION, 2 * KEYVAL_HEADS * HEAD_DIMENSION), 0.001, 0.006, ((0, 512),), jnp.float32)
    keyval_first_moment = noise(key_of[9], (MODEL_DIMENSION, 2 * KEYVAL_HEADS * HEAD_DIMENSION), 0.001, 0.006, ((0, 512),), jnp.float32)
    keyval_second_moment = jnp.clip(jnp.exp(math.log(9.999999747378752e-06) - 4.6051701 * jax.random.uniform(key_of[10], (MODEL_DIMENSION, 2 * KEYVAL_HEADS * HEAD_DIMENSION), jnp.float32) ** block_scale(key_of[10], (MODEL_DIMENSION, 2 * KEYVAL_HEADS * HEAD_DIMENSION), ((0, 512),), -0.2, 0.2)), 1.0000000116860974e-07, 9.999999747378752e-06)
    output_param = noise(key_of[11], (MODEL_DIMENSION, QUERY_HEADS_LOCAL * HEAD_DIMENSION), (4 * HEAD_DIMENSION) ** -0.5, 0.25, ((0, 512),), jnp.float32)
    output_grad = noise(key_of[12], (MODEL_DIMENSION, QUERY_HEADS_LOCAL * HEAD_DIMENSION), 0.001, 0.006, ((0, 512),), jnp.float32)
    output_moment = noise(key_of[13], (MODEL_DIMENSION, QUERY_HEADS_LOCAL * HEAD_DIMENSION), 0.001, 0.006, ((0, 512),), jnp.float32)
    output_second = jnp.clip(jnp.exp(math.log(9.999999747378752e-06) - 4.6051701 * jax.random.uniform(key_of[14], (MODEL_DIMENSION, QUERY_HEADS_LOCAL * HEAD_DIMENSION), jnp.float32) ** block_scale(key_of[14], (MODEL_DIMENSION, QUERY_HEADS_LOCAL * HEAD_DIMENSION), ((0, 512),), -0.2, 0.2)), 1.0000000116860974e-07, 9.999999747378752e-06)
    return {"hidden": hidden, "norm_gain": norm_gain, "lengths": lengths, "query_param": query_param, "query_grad": query_grad, "query_moment": query_moment, "query_second": query_second, "keyval_param": keyval_param, "keyval_gradient": keyval_gradient, "keyval_first_moment": keyval_first_moment, "keyval_second_moment": keyval_second_moment, "output_param": output_param, "output_grad": output_grad, "output_moment": output_moment, "output_second": output_second}


learn_rate = 0.015
beta_one = 0.5
beta_two = 0.9
adam_step = 1000.0
adam_eps = 1e-08
decay_rate = 0.1
norm_eps = 1e-06
rope_base = 1000000.0
masked_score = -1e+30

def adam_update(current, gradient, moment, second):
    moment_new = beta_one * moment + (1.0 - beta_one) * gradient
    second_new = beta_two * second + (1.0 - beta_two) * gradient * gradient
    corrected = moment_new / (1.0 - beta_one ** adam_step)
    denominator = jnp.sqrt(second_new / (1.0 - beta_two ** adam_step)) + adam_eps
    return (current - learn_rate * (corrected / denominator + decay_rate * current)).astype(jnp.bfloat16)

def normalize(hidden, norm_gain):
    values = hidden.astype(jnp.float32)
    factor = lax.rsqrt(lax.optimization_barrier(jnp.mean(values * values, axis=-1, keepdims=True)) + norm_eps)
    return (values * factor * norm_gain).astype(jnp.bfloat16)

def rotary_embed(values, token_positions):
    half_width = values.shape[-1] // 2
    frequency = rope_base ** (-jnp.arange(half_width, dtype=jnp.float32) * 2.0 / values.shape[-1])
    angles = token_positions.astype(jnp.float32)[:, None] * frequency[None, :]
    cosine_table = jnp.concatenate([jnp.cos(angles), jnp.cos(angles)], axis=-1)
    sine_table = jnp.concatenate([jnp.sin(angles), jnp.sin(angles)], axis=-1)
    first_half = values[..., :half_width]
    second_half = values[..., half_width:]
    rotated = jnp.concatenate([-second_half, first_half], axis=-1)
    return values * cosine_table + rotated * sine_table

def prompt_layer(normed, length, query_weight, keyval_matrix, output_weight):
    queries = jnp.dot(normed, query_weight, preferred_element_type=jnp.float32)
    keyval_outputs = jnp.dot(normed, keyval_matrix, preferred_element_type=jnp.float32)
    token_positions = jnp.arange(PROMPT_LENGTH)
    query_heads = rotary_embed(queries.reshape(PROMPT_LENGTH, QUERY_HEADS_LOCAL, HEAD_DIMENSION).transpose(1, 0, 2), token_positions).astype(jnp.bfloat16)
    key_head_rows = rotary_embed(keyval_outputs[:, :KEYVAL_HEADS * HEAD_DIMENSION].reshape(PROMPT_LENGTH, KEYVAL_HEADS, HEAD_DIMENSION).transpose(1, 0, 2), token_positions).astype(jnp.bfloat16)
    value_head_rows = keyval_outputs[:, KEYVAL_HEADS * HEAD_DIMENSION:].reshape(PROMPT_LENGTH, KEYVAL_HEADS, HEAD_DIMENSION).transpose(1, 0, 2).astype(jnp.bfloat16)
    group_width = QUERY_HEADS_LOCAL // KEYVAL_HEADS
    key_full = jnp.repeat(key_head_rows, group_width, axis=0)
    value_full = jnp.repeat(value_head_rows, group_width, axis=0)
    scores = jnp.einsum('hqd,hkd->hqk', query_heads.astype(jnp.float32), key_full.astype(jnp.float32)) / math.sqrt(HEAD_DIMENSION)
    allowed = (token_positions[None, :] <= token_positions[:, None]) & (token_positions[None, :] < length)
    scores = jnp.where(allowed[None], scores, masked_score)
    row_max = lax.optimization_barrier(jnp.max(scores, axis=-1, keepdims=True))
    exponent = jnp.exp(scores - row_max)
    attention = (exponent / lax.optimization_barrier(jnp.sum(exponent, axis=-1, keepdims=True))).astype(jnp.bfloat16)
    head_out = jnp.einsum('hqk,hkd->hqd', attention.astype(jnp.float32), value_full.astype(jnp.float32)).astype(jnp.bfloat16)
    head_out = head_out.transpose(1, 0, 2).reshape(PROMPT_LENGTH, QUERY_HEADS_LOCAL * HEAD_DIMENSION)
    group_cols = QUERY_HEADS_LOCAL * HEAD_DIMENSION // N_TENSOR
    head_groups = head_out.reshape(PROMPT_LENGTH, N_TENSOR, group_cols).transpose(1, 0, 2)
    weight_groups = output_weight.reshape(MODEL_DIMENSION, N_TENSOR, group_cols).transpose(1, 0, 2)

    def add_group(totals, sliced):
        head_part, weight_part = sliced
        partial_term = lax.dot_general(head_part, weight_part, (((1,), (1,)), ((), ())), preferred_element_type=jnp.float32)
        return (totals + partial_term.astype(jnp.bfloat16).astype(jnp.float32), None)
    summed, unused = lax.scan(add_group, jnp.zeros((PROMPT_LENGTH, MODEL_DIMENSION), jnp.float32), (head_groups, weight_groups))
    return summed.astype(jnp.bfloat16)

def reference(hidden, norm_gain, lengths, query_param, query_grad, query_moment, query_second, keyval_param, keyval_gradient, keyval_first_moment, keyval_second_moment, output_param, output_grad, output_moment, output_second):
    query_weight = adam_update(query_param, query_grad, query_moment, query_second)
    keyval_matrix = adam_update(keyval_param, keyval_gradient, keyval_first_moment, keyval_second_moment)
    output_weight = adam_update(output_param, output_grad, output_moment, output_second)
    normed = normalize(hidden, norm_gain)

    def one_prompt(packed):
        return prompt_layer(packed[0], packed[1], query_weight, keyval_matrix, output_weight)
    return lax.map(one_prompt, (normed, lengths))
```

```python
import math

import jax
import jax.numpy as jnp
from jax import lax
from jax.sharding import Mesh, PartitionSpec as P

XL = ("x", "l")
HC = ("h", "c")
XLH = ("x", "l", "h")

QUERY_HEADS_LOCAL = 32
KEYVAL_HEADS = 4
HEAD_DIMENSION = 128

learn_rate = 0.015
beta_one = 0.5
beta_two = 0.9
adam_step = 1000.0
adam_eps = 1e-08
decay_rate = 0.1
norm_eps = 1e-06
rope_base = 1000000.0
masked_score = -1e30


def adam_update(current, gradient, moment, second):
    moment_new = beta_one * moment + (1.0 - beta_one) * gradient
    second_new = beta_two * second + (1.0 - beta_two) * gradient * gradient
    corrected = moment_new / (1.0 - beta_one**adam_step)
    denominator = jnp.sqrt(second_new / (1.0 - beta_two**adam_step)) + adam_eps
    return (current - learn_rate * (corrected / denominator + decay_rate * current)).astype(
        jnp.bfloat16
    )


def normalize(hidden, norm_gain):
    values = hidden.astype(jnp.float32)
    factor = lax.rsqrt(jnp.mean(values * values, axis=-1, keepdims=True) + norm_eps)
    return (values * factor * norm_gain).astype(jnp.bfloat16)


def swap_blocks(blocks, axes):
    return lax.all_to_all(blocks, axes, split_axis=0, concat_axis=0, tiled=True)


def partner(values):
    return lax.ppermute(values, "c", [(0, 1), (1, 0)])


def on_device(
    hidden,
    norm_gain,
    lengths,
    query_param,
    query_grad,
    query_moment,
    query_second,
    keyval_param,
    keyval_gradient,
    keyval_first_moment,
    keyval_second_moment,
    output_param,
    output_grad,
    output_moment,
    output_second,
):
    bf16, f32 = jnp.bfloat16, jnp.float32
    xl = lax.axis_size(XL)
    hc = lax.axis_size(HC)
    n_h, n_c, n_z = lax.axis_size("h"), lax.axis_size("c"), lax.axis_size("z")
    tokens, width = hidden.shape[1], hidden.shape[2]
    rows = query_param.shape[0]
    heads = QUERY_HEADS_LOCAL // hc
    head_cols = heads * HEAD_DIMENSION
    depth = width // xl

    query_weight = adam_update(query_param, query_grad, query_moment, query_second)
    keyval_weight = adam_update(
        keyval_param, keyval_gradient, keyval_first_moment, keyval_second_moment
    )
    query_blocks = query_weight.reshape(rows, hc, head_cols).transpose(1, 0, 2)
    keyval_blocks = (
        keyval_weight.reshape(rows, 2, KEYVAL_HEADS, HEAD_DIMENSION)
        .transpose(2, 0, 1, 3)
        .reshape(KEYVAL_HEADS, rows, 2 * HEAD_DIMENSION)
    )
    keyval_blocks = jnp.repeat(keyval_blocks, hc // KEYVAL_HEADS, axis=0)
    proj_blocks = swap_blocks(jnp.concatenate([query_blocks, keyval_blocks], axis=2), HC)
    proj_cols = proj_blocks.shape[2]
    proj_all = lax.all_gather(proj_blocks, "z", axis=0)
    proj_weight = (
        proj_all.reshape(n_z, n_h, n_c, rows, proj_cols)
        .transpose(2, 1, 0, 3, 4)
        .reshape(depth, proj_cols)
    )
    output_weight = adam_update(output_param, output_grad, output_moment, output_second)
    output_blocks = swap_blocks(
        output_weight.reshape(rows, hc, head_cols).transpose(1, 0, 2), HC
    )
    output_all = lax.all_gather(output_blocks, "z", axis=0)
    output_matrix = (
        output_all.reshape(n_z, n_h, n_c, rows, head_cols)
        .transpose(2, 1, 0, 3, 4)
        .reshape(depth, head_cols)
    )

    local_rows = normalize(hidden[0], norm_gain)
    row_blocks = local_rows.reshape(tokens, xl, 1, depth).transpose(1, 2, 0, 3)
    row_blocks = jnp.broadcast_to(row_blocks, (xl, n_h, tokens, depth))
    row_blocks = swap_blocks(row_blocks.reshape(xl * n_h, tokens, depth), XLH)
    here = row_blocks.reshape(xl, 1, n_h * tokens, depth)
    both = jnp.concatenate([here, partner(here)], axis=1)
    spread = n_c * n_h * tokens

    partial = jnp.dot(
        both.reshape(xl * spread, depth), proj_weight, preferred_element_type=f32
    ).astype(bf16)
    partial = swap_blocks(partial.reshape(xl, spread, proj_cols), XL)
    projected = jnp.sum(partial.astype(f32), axis=0).reshape(n_c, n_h * tokens, proj_cols)

    half = HEAD_DIMENSION // 2
    frequency = rope_base ** (-jnp.arange(half, dtype=f32) * 2.0 / HEAD_DIMENSION)
    local = jnp.arange(n_h * tokens)
    stride = n_z * tokens
    positions = (local // tokens) * stride + lax.axis_index("z") * tokens + local % tokens
    angles = positions.astype(f32)[:, None] * frequency[None, :]
    cosine = jnp.concatenate([jnp.cos(angles), jnp.cos(angles)], axis=-1)
    sine = jnp.concatenate([-jnp.sin(angles), jnp.sin(angles)], axis=-1)

    def rotary(values):
        swapped = jnp.concatenate([values[..., half:], values[..., :half]], axis=-1)
        return (values * cosine + swapped * sine).astype(bf16)

    key_rows = rotary(projected[:, :, head_cols : head_cols + HEAD_DIMENSION])
    value_rows = projected[:, :, head_cols + HEAD_DIMENSION :].astype(bf16)
    keyval_rows = jnp.concatenate([key_rows, value_rows], axis=-1)
    keyval_rows = swap_blocks(
        jnp.broadcast_to(keyval_rows[None], (n_z,) + keyval_rows.shape), "z"
    )
    keyval_rows = keyval_rows.transpose(1, 0, 2, 3).reshape(
        n_c, n_z * n_h * tokens, 2 * HEAD_DIMENSION
    )
    query_rows = jnp.concatenate(
        [
            rotary(projected[:, :, i * HEAD_DIMENSION : (i + 1) * HEAD_DIMENSION])
            for i in range(heads)
        ],
        axis=1,
    )

    scores = jnp.einsum(
        "cqd,ckd->cqk",
        query_rows,
        keyval_rows[:, :, :HEAD_DIMENSION],
        preferred_element_type=f32,
    ) / math.sqrt(HEAD_DIMENSION)
    key_at = jnp.arange(n_z * n_h * tokens)
    key_at = (
        (key_at // tokens % n_h) * stride + key_at // (n_h * tokens) * tokens + key_at % tokens
    )
    query_at = jnp.tile(positions, heads)
    valid = jnp.stack([lengths[0], partner(lengths)[0]])
    allowed = (key_at[None, :] <= query_at[:, None])[None] & (
        key_at[None, None, :] < valid[:, None, None]
    )
    scores = jnp.where(allowed, scores, masked_score)
    exponent = jnp.exp(scores - jnp.max(scores, axis=-1, keepdims=True))
    attention = (exponent / jnp.sum(exponent, axis=-1, keepdims=True)).astype(bf16)
    head_out = jnp.einsum(
        "cqk,ckd->cqd",
        attention,
        keyval_rows[:, :, HEAD_DIMENSION:],
        preferred_element_type=f32,
    ).astype(bf16)
    head_out = (
        head_out.reshape(n_c, heads, n_h * tokens, HEAD_DIMENSION)
        .transpose(0, 2, 1, 3)
        .reshape(spread, head_cols)
    )

    head_all = swap_blocks(jnp.broadcast_to(head_out[None], (xl,) + head_out.shape), XL)
    mixed = lax.dot_general(
        head_all.reshape(xl * spread, head_cols),
        output_matrix,
        (((1,), (1,)), ((), ())),
        preferred_element_type=f32,
    ).reshape(xl, n_c, n_h * tokens, depth)
    mixed = (mixed[:, 0] + partner(mixed[:, 1].astype(bf16)).astype(f32)).astype(bf16)
    mixed = swap_blocks(mixed.reshape(xl * n_h, tokens, depth), XLH)
    mixed = jnp.sum(mixed.reshape(xl, n_h, tokens, depth).astype(f32), axis=1).astype(bf16)
    return mixed.transpose(1, 0, 2).reshape(1, tokens, width)


def solution(mesh):
    fine = Mesh(mesh.devices.reshape(4, 2, 2, 4, 8), ("x", "l", "c", "h", "z"))
    section, tensor = ("x", "l", "c"), ("h", "z")
    by_row = P(section + tensor, None)
    return jax.shard_map(
        on_device,
        mesh=fine,
        in_specs=(P(section, tensor, None), P(), P(section)) + (by_row,) * 12,
        out_specs=P(section, tensor, None),
        check_vma=False,
    )
```

```python
import math

import jax
import jax.numpy as jnp
from jax import lax
from jax.sharding import Mesh, PartitionSpec as P

XL = ("x", "l")
HC = ("h", "c")
XLH = ("x", "l", "h")

QUERY_HEADS_LOCAL = 32
KEYVAL_HEADS = 4
HEAD_DIMENSION = 128

learn_rate = 0.015
beta_one = 0.5
beta_two = 0.9
adam_step = 1000.0
adam_eps = 1e-08
decay_rate = 0.1
norm_eps = 1e-06
rope_base = 1000000.0
masked_score = -1e30


def adam_update(current, gradient, moment, second):
    moment_new = beta_one * moment + (1.0 - beta_one) * gradient
    second_new = beta_two * second + (1.0 - beta_two) * gradient * gradient
    corrected = moment_new / (1.0 - beta_one**adam_step)
    denominator = jnp.sqrt(second_new / (1.0 - beta_two**adam_step)) + adam_eps
    return (current - learn_rate * (corrected / denominator + decay_rate * current)).astype(
        jnp.bfloat16
    )


def normalize(hidden, norm_gain):
    values = hidden.astype(jnp.float32)
    factor = lax.rsqrt(jnp.mean(values * values, axis=-1, keepdims=True) + norm_eps)
    return (values * factor * norm_gain).astype(jnp.bfloat16)


def swap_blocks(blocks, axes):
    return lax.all_to_all(blocks, axes, split_axis=0, concat_axis=0, tiled=True)


def partner(values):
    return lax.ppermute(values, "c", [(0, 1), (1, 0)])


def on_device(
    hidden,
    norm_gain,
    lengths,
    query_param,
    query_grad,
    query_moment,
    query_second,
    keyval_param,
    keyval_gradient,
    keyval_first_moment,
    keyval_second_moment,
    output_param,
    output_grad,
    output_moment,
    output_second,
):
    bf16, f32 = jnp.bfloat16, jnp.float32
    xl = lax.axis_size(XL)
    hc = lax.axis_size(HC)
    n_h, n_c, n_z = lax.axis_size("h"), lax.axis_size("c"), lax.axis_size("z")
    tokens, width = hidden.shape[1], hidden.shape[2]
    rows = query_param.shape[0]
    heads = QUERY_HEADS_LOCAL // hc
    head_cols = heads * HEAD_DIMENSION
    depth = width // xl

    query_weight = adam_update(query_param, query_grad, query_moment, query_second)
    keyval_weight = adam_update(
        keyval_param, keyval_gradient, keyval_first_moment, keyval_second_moment
    )
    output_weight = adam_update(output_param, output_grad, output_moment, output_second)
    proj_cols = head_cols + HEAD_DIMENSION
    weight_blocks = jnp.concatenate(
        [
            query_weight.reshape(rows, hc, head_cols).transpose(1, 0, 2),
            keyval_weight.reshape(rows, n_c, n_h, HEAD_DIMENSION)
            .transpose(2, 1, 0, 3)
            .reshape(hc, rows, HEAD_DIMENSION),
            output_weight.reshape(rows, hc, head_cols).transpose(1, 0, 2),
            jnp.broadcast_to(lengths[0].astype(bf16), (hc, rows, HEAD_DIMENSION)),
        ],
        axis=2,
    )
    weight_blocks = swap_blocks(weight_blocks, HC)
    proj_all = lax.all_gather(weight_blocks[:, :, :proj_cols], "z", axis=0)
    proj_weight = (
        proj_all.reshape(n_z, n_h, n_c, rows, proj_cols)
        .transpose(2, 1, 0, 3, 4)
        .reshape(depth, proj_cols)
    )
    output_all = lax.all_gather(
        weight_blocks[:, :, proj_cols : proj_cols + head_cols], "z", axis=0
    )
    output_matrix = (
        output_all.reshape(n_z, n_h, n_c, rows, head_cols)
        .transpose(2, 1, 0, 3, 4)
        .reshape(depth, head_cols)
    )
    own_length = lengths[0]
    pair_lengths = weight_blocks[:n_c, 0, proj_cols + head_cols].astype(jnp.int32)
    valid = jnp.stack([own_length, jnp.sum(pair_lengths) - own_length])

    local_rows = normalize(hidden[0], norm_gain)
    row_blocks = local_rows.reshape(tokens, xl, 1, depth).transpose(1, 2, 0, 3)
    row_blocks = jnp.broadcast_to(row_blocks, (xl, n_h, tokens, depth))
    row_blocks = swap_blocks(row_blocks.reshape(xl * n_h, tokens, depth), XLH)
    here = row_blocks.reshape(xl, 1, n_h * tokens, depth)
    both = jnp.concatenate([here, partner(here)], axis=1)
    spread = n_c * n_h * tokens

    partial = jnp.dot(
        both.reshape(xl * spread, depth), proj_weight, preferred_element_type=f32
    ).astype(bf16)
    partial = swap_blocks(partial.reshape(xl, spread, proj_cols), XL)
    projected = jnp.sum(partial.astype(f32), axis=0).reshape(n_c, n_h * tokens, proj_cols)

    half = HEAD_DIMENSION // 2
    frequency = rope_base ** (-jnp.arange(half, dtype=f32) * 2.0 / HEAD_DIMENSION)
    local = jnp.arange(n_h * tokens)
    stride = n_z * tokens
    positions = (local // tokens) * stride + lax.axis_index("z") * tokens + local % tokens
    angles = positions.astype(f32)[:, None] * frequency[None, :]
    cosine = jnp.concatenate([jnp.cos(angles), jnp.cos(angles)], axis=-1)
    sine = jnp.concatenate([-jnp.sin(angles), jnp.sin(angles)], axis=-1)

    def rotary(values):
        swapped = jnp.concatenate([values[..., half:], values[..., :half]], axis=-1)
        return (values * cosine + swapped * sine).astype(bf16)

    side = lax.axis_index("c")
    keyval_rows = projected[:, :, head_cols:]
    keyval_rows = jnp.where(side == 0, rotary(keyval_rows), keyval_rows.astype(bf16))
    to_side = (jnp.arange(n_c) == side)[None, :, None, None, None]
    keyval_rows = jnp.where(
        jnp.broadcast_to(to_side, (n_z, n_c) + keyval_rows.shape),
        keyval_rows[None, None],
        keyval_rows[::-1][None, None],
    )
    keyval_rows = swap_blocks(
        keyval_rows.reshape(n_z * n_c, n_c, n_h * tokens, HEAD_DIMENSION), ("z", "c")
    )
    keyval_rows = (
        keyval_rows.reshape(n_z, n_c, n_c, n_h * tokens, HEAD_DIMENSION)
        .transpose(1, 2, 0, 3, 4)
        .reshape(n_c, n_c, n_z * n_h * tokens, HEAD_DIMENSION)
    )
    query_rows = jnp.concatenate(
        [
            rotary(projected[:, :, i * HEAD_DIMENSION : (i + 1) * HEAD_DIMENSION])
            for i in range(heads)
        ],
        axis=1,
    )

    scores = jnp.einsum(
        "cqd,ckd->cqk",
        query_rows,
        keyval_rows[0],
        preferred_element_type=f32,
    ) / math.sqrt(HEAD_DIMENSION)
    key_at = jnp.arange(n_z * n_h * tokens)
    key_at = (
        (key_at // tokens % n_h) * stride + key_at // (n_h * tokens) * tokens + key_at % tokens
    )
    query_at = jnp.tile(positions, heads)
    allowed = (key_at[None, :] <= query_at[:, None])[None] & (
        key_at[None, None, :] < valid[:, None, None]
    )
    scores = jnp.where(allowed, scores, masked_score)
    exponent = jnp.exp(scores - jnp.max(scores, axis=-1, keepdims=True))
    attention = (exponent / jnp.sum(exponent, axis=-1, keepdims=True)).astype(bf16)
    head_out = jnp.einsum(
        "cqk,ckd->cqd",
        attention,
        keyval_rows[1],
        preferred_element_type=f32,
    ).astype(bf16)
    head_out = (
        head_out.reshape(n_c, heads, n_h * tokens, HEAD_DIMENSION)
        .transpose(0, 2, 1, 3)
        .reshape(spread, head_cols)
    )

    head_all = swap_blocks(jnp.broadcast_to(head_out[None], (xl,) + head_out.shape), XL)
    mixed = lax.dot_general(
        head_all.reshape(xl * spread, head_cols),
        output_matrix,
        (((1,), (1,)), ((), ())),
        preferred_element_type=f32,
    ).reshape(xl, n_c, n_h * tokens, depth)
    mixed = (mixed[:, 0] + partner(mixed[:, 1].astype(bf16)).astype(f32)).astype(bf16)
    mixed = swap_blocks(mixed.reshape(xl * n_h, tokens, depth), XLH)
    mixed = jnp.sum(mixed.reshape(xl, n_h, tokens, depth).astype(f32), axis=1).astype(bf16)
    return mixed.transpose(1, 0, 2).reshape(1, tokens, width)


def solution(mesh):
    fine = Mesh(mesh.devices.reshape(4, 2, 2, 4, 8), ("x", "l", "c", "h", "z"))
    section, tensor = ("x", "l", "c"), ("h", "z")
    by_row = P(section + tensor, None)
    return jax.shard_map(
        on_device,
        mesh=fine,
        in_specs=(P(section, tensor, None), P(), P(section)) + (by_row,) * 12,
        out_specs=P(section, tensor, None),
        check_vma=False,
    )
```

```python
import math

import jax
import jax.numpy as jnp
from jax import lax
from jax.sharding import Mesh, PartitionSpec as P

XL = ("x", "l")
CH = ("c", "h")
XLH = ("x", "l", "h")

QUERY_HEADS_LOCAL = 32
KEYVAL_HEADS = 4
HEAD_DIMENSION = 128

learn_rate = 0.015
beta_one = 0.5
beta_two = 0.9
adam_step = 1000.0
adam_eps = 1e-08
decay_rate = 0.1
norm_eps = 1e-06
rope_base = 1000000.0
masked_score = -1e30


def adam_update(current, gradient, moment, second):
    moment_new = beta_one * moment + (1.0 - beta_one) * gradient
    second_new = beta_two * second + (1.0 - beta_two) * gradient * gradient
    corrected = moment_new / (1.0 - beta_one**adam_step)
    denominator = jnp.sqrt(second_new / (1.0 - beta_two**adam_step)) + adam_eps
    return (current - learn_rate * (corrected / denominator + decay_rate * current)).astype(
        jnp.bfloat16
    )


def normalize(hidden, norm_gain):
    values = hidden.astype(jnp.float32)
    factor = lax.rsqrt(jnp.mean(values * values, axis=-1, keepdims=True) + norm_eps)
    return (values * factor * norm_gain).astype(jnp.bfloat16)


def swap_blocks(blocks, axes):
    return lax.all_to_all(blocks, axes, split_axis=0, concat_axis=0, tiled=True)


def partner(values):
    return lax.ppermute(values, "c", [(0, 1), (1, 0)])


def gather_z(values, size):
    blocks = [values]
    for d in range(1, size):
        blocks.append(lax.ppermute(values, "z", [(i, (i - d) % size) for i in range(size)]))
    return jnp.stack(blocks, axis=1)


def roll_lanes(values, steps, unit, count):
    shift = count // 2
    while shift:
        cut = shift * unit
        moved = jnp.concatenate([values[..., cut:], values[..., :cut]], axis=-1)
        values = jnp.where((steps // shift) % 2 == 1, moved, values)
        shift //= 2
    return values


def on_device(
    hidden,
    norm_gain,
    lengths,
    query_param,
    query_grad,
    query_moment,
    query_second,
    keyval_param,
    keyval_gradient,
    keyval_first_moment,
    keyval_second_moment,
    output_param,
    output_grad,
    output_moment,
    output_second,
):
    bf16, f32 = jnp.bfloat16, jnp.float32
    xl = lax.axis_size(XL)
    hc = lax.axis_size(CH)
    n_h, n_c, n_z = lax.axis_size("h"), lax.axis_size("c"), lax.axis_size("z")
    tokens, width = hidden.shape[1], hidden.shape[2]
    rows = query_param.shape[0]
    heads = QUERY_HEADS_LOCAL // hc
    head_cols = heads * HEAD_DIMENSION
    depth = width // xl

    query_weight = adam_update(query_param, query_grad, query_moment, query_second)
    keyval_weight = adam_update(
        keyval_param, keyval_gradient, keyval_first_moment, keyval_second_moment
    )
    output_weight = adam_update(output_param, output_grad, output_moment, output_second)
    proj_cols = head_cols + HEAD_DIMENSION

    def by_slice(weight):
        return weight.reshape(rows, n_h, n_c, head_cols).transpose(2, 1, 0, 3)

    weight_blocks = jnp.concatenate(
        [
            by_slice(query_weight),
            keyval_weight.reshape(rows, n_c, n_h, HEAD_DIMENSION).transpose(1, 2, 0, 3),
            by_slice(output_weight),
            jnp.broadcast_to(lengths[0].astype(bf16), (n_c, n_h, rows, HEAD_DIMENSION)),
        ],
        axis=3,
    ).reshape(hc, rows, -1)
    weight_blocks = swap_blocks(weight_blocks, CH)
    proj_weight = gather_z(weight_blocks[:, :, :proj_cols], n_z).reshape(depth, proj_cols)
    output_matrix = gather_z(
        weight_blocks[:, :, proj_cols : proj_cols + head_cols], n_z
    ).reshape(depth, head_cols)
    own_length = lengths[0]
    pair_lengths = weight_blocks[:: n_h, 0, proj_cols + head_cols].astype(jnp.int32)
    valid = jnp.stack([own_length, jnp.sum(pair_lengths) - own_length])
    here_z = lax.axis_index("z")

    local_rows = normalize(hidden[0], norm_gain)
    local_rows = roll_lanes(local_rows.reshape(tokens, -1, n_z * rows), here_z, rows, n_z)
    row_blocks = local_rows.reshape(tokens, xl, 1, depth).transpose(1, 2, 0, 3)
    row_blocks = jnp.broadcast_to(row_blocks, (xl, n_h, tokens, depth))
    row_blocks = swap_blocks(row_blocks.reshape(xl * n_h, tokens, depth), XLH)
    here = row_blocks.reshape(xl, 1, n_h * tokens, depth)
    both = jnp.concatenate([here, partner(here)], axis=1)
    spread = n_c * n_h * tokens

    partial = jnp.dot(
        both.reshape(xl * spread, depth), proj_weight, preferred_element_type=f32
    ).astype(bf16)
    partial = swap_blocks(partial.reshape(xl, spread, proj_cols), XL)
    projected = jnp.sum(partial.astype(f32), axis=0).reshape(n_c, n_h * tokens, proj_cols)

    half = HEAD_DIMENSION // 2
    frequency = rope_base ** (-jnp.arange(half, dtype=f32) * 2.0 / HEAD_DIMENSION)
    local = jnp.arange(n_h * tokens)
    stride = n_z * tokens
    positions = (local // tokens) * stride + here_z * tokens + local % tokens
    angles = positions.astype(f32)[:, None] * frequency[None, :]
    cosine = jnp.concatenate([jnp.cos(angles), jnp.cos(angles)], axis=-1)
    sine = jnp.concatenate([-jnp.sin(angles), jnp.sin(angles)], axis=-1)

    def rotary(values):
        swapped = jnp.concatenate([values[..., half:], values[..., :half]], axis=-1)
        return (values * cosine + swapped * sine).astype(bf16)

    side = lax.axis_index("c")
    keyval_rows = projected[:, :, head_cols:]
    keyval_rows = jnp.where(side == 0, rotary(keyval_rows), keyval_rows.astype(bf16))
    to_side = (jnp.arange(n_c) == side)[None, :, None, None, None]
    keyval_rows = jnp.where(
        jnp.broadcast_to(to_side, (n_z, n_c) + keyval_rows.shape),
        keyval_rows[None, None],
        keyval_rows[::-1][None, None],
    )
    keyval_rows = swap_blocks(
        keyval_rows.reshape(n_z * n_c, n_c, n_h * tokens, HEAD_DIMENSION), ("z", "c")
    )
    keyval_rows = (
        keyval_rows.reshape(n_z, n_c, n_c, n_h * tokens, HEAD_DIMENSION)
        .transpose(1, 2, 0, 3, 4)
        .reshape(n_c, n_c, n_z * n_h * tokens, HEAD_DIMENSION)
    )
    query_rows = jnp.concatenate(
        [
            rotary(projected[:, :, i * HEAD_DIMENSION : (i + 1) * HEAD_DIMENSION])
            for i in range(heads)
        ],
        axis=1,
    )

    scores = jnp.einsum(
        "cqd,ckd->cqk",
        query_rows,
        keyval_rows[0],
        preferred_element_type=f32,
    ) / math.sqrt(HEAD_DIMENSION)
    key_at = jnp.arange(n_z * n_h * tokens)
    key_at = (
        (key_at // tokens % n_h) * stride + key_at // (n_h * tokens) * tokens + key_at % tokens
    )
    query_at = jnp.tile(positions, heads)
    allowed = (key_at[None, :] <= query_at[:, None])[None] & (
        key_at[None, None, :] < valid[:, None, None]
    )
    scores = jnp.where(allowed, scores, masked_score)
    exponent = jnp.exp(scores - jnp.max(scores, axis=-1, keepdims=True))
    attention = (exponent / jnp.sum(exponent, axis=-1, keepdims=True)).astype(bf16)
    head_out = jnp.einsum(
        "cqk,ckd->cqd",
        attention,
        keyval_rows[1],
        preferred_element_type=f32,
    ).astype(bf16)
    head_out = (
        head_out.reshape(n_c, heads, n_h * tokens, HEAD_DIMENSION)
        .transpose(0, 2, 1, 3)
        .reshape(spread, head_cols)
    )

    head_all = swap_blocks(jnp.broadcast_to(head_out[None], (xl,) + head_out.shape), XL)
    mixed = lax.dot_general(
        head_all.reshape(xl * spread, head_cols),
        output_matrix,
        (((1,), (1,)), ((), ())),
        preferred_element_type=f32,
    ).reshape(xl, n_c, n_h * tokens, depth)
    mixed = (mixed[:, 0] + partner(mixed[:, 1].astype(bf16)).astype(f32)).astype(bf16)
    mixed = swap_blocks(mixed.reshape(xl * n_h, tokens, depth), XLH)
    mixed = jnp.sum(mixed.reshape(xl, n_h, tokens, depth).astype(f32), axis=1).astype(bf16)
    mixed = mixed.transpose(1, 0, 2).reshape(tokens, -1, n_z * rows)
    mixed = roll_lanes(mixed, (n_z - here_z) % n_z, rows, n_z)
    return mixed.reshape(1, tokens, width)


def solution(mesh):
    fine = Mesh(mesh.devices.reshape(4, 2, 2, 4, 8), ("x", "l", "c", "h", "z"))
    section, tensor = ("x", "l", "c"), ("h", "z")
    by_row = P(section + tensor, None)
    return jax.shard_map(
        on_device,
        mesh=fine,
        in_specs=(P(section, tensor, None), P(), P(section)) + (by_row,) * 12,
        out_specs=P(section, tensor, None),
        check_vma=False,
    )
```

```python
import math

import jax
import jax.numpy as jnp
from jax import lax
from jax.sharding import Mesh, PartitionSpec as P

XL = ("x", "l")
CZ = ("c", "z")
XLH = ("x", "l", "h")

QUERY_HEADS_LOCAL = 32
KEYVAL_HEADS = 4
HEAD_DIMENSION = 128

learn_rate = 0.015
beta_one = 0.5
beta_two = 0.9
adam_step = 1000.0
adam_eps = 1e-08
decay_rate = 0.1
norm_eps = 1e-06
rope_base = 1000000.0
masked_score = -1e30


def adam_update(current, gradient, moment, second):
    moment_new = beta_one * moment + (1.0 - beta_one) * gradient
    second_new = beta_two * second + (1.0 - beta_two) * gradient * gradient
    corrected = moment_new / (1.0 - beta_one**adam_step)
    denominator = jnp.sqrt(second_new / (1.0 - beta_two**adam_step)) + adam_eps
    return (current - learn_rate * (corrected / denominator + decay_rate * current)).astype(
        jnp.bfloat16
    )


def normalize(hidden, norm_gain):
    values = hidden.astype(jnp.float32)
    factor = lax.rsqrt(jnp.mean(values * values, axis=-1, keepdims=True) + norm_eps)
    return (values * factor * norm_gain).astype(jnp.bfloat16)


def swap_blocks(blocks, axes):
    return lax.all_to_all(blocks, axes, split_axis=0, concat_axis=0, tiled=True)


def regroup(values, n_h, n_z, unit):
    size = n_h * n_z * unit
    target = lax.broadcasted_iota(jnp.int32, (size, size), 1)
    source = (
        target // unit % n_h * (n_z * unit) + target // (unit * n_h) * unit + target % unit
    )
    matrix = (lax.broadcasted_iota(jnp.int32, (size, size), 0) == source).astype(jnp.bfloat16)
    return jnp.dot(values, matrix, preferred_element_type=jnp.float32).astype(jnp.bfloat16)


def on_device(
    hidden,
    norm_gain,
    lengths,
    query_param,
    query_grad,
    query_moment,
    query_second,
    keyval_param,
    keyval_gradient,
    keyval_first_moment,
    keyval_second_moment,
    output_param,
    output_grad,
    output_moment,
    output_second,
):
    bf16, f32 = jnp.bfloat16, jnp.float32
    xl = lax.axis_size(XL)
    n_h, n_c, n_z = lax.axis_size("h"), lax.axis_size("c"), lax.axis_size("z")
    tokens, width = hidden.shape[1], hidden.shape[2]
    rows = query_param.shape[0]
    heads = QUERY_HEADS_LOCAL // n_h
    head_cols = heads * HEAD_DIMENSION
    depth = width // xl

    query_weight = adam_update(query_param, query_grad, query_moment, query_second)
    keyval_weight = adam_update(
        keyval_param, keyval_gradient, keyval_first_moment, keyval_second_moment
    )
    proj_blocks = jnp.concatenate(
        [
            query_weight.reshape(rows, n_h, head_cols).transpose(1, 0, 2),
            keyval_weight[:, : n_h * HEAD_DIMENSION]
            .reshape(rows, n_h, HEAD_DIMENSION)
            .transpose(1, 0, 2),
            keyval_weight[:, n_h * HEAD_DIMENSION :]
            .reshape(rows, n_h, HEAD_DIMENSION)
            .transpose(1, 0, 2),
        ],
        axis=2,
    )
    proj_cols = proj_blocks.shape[2]
    proj_all = lax.all_gather(swap_blocks(proj_blocks, "h"), CZ, axis=0)
    proj_weight = proj_all.reshape(depth, proj_cols)
    output_weight = adam_update(output_param, output_grad, output_moment, output_second)
    output_blocks = output_weight.reshape(rows, n_h, head_cols).transpose(1, 0, 2)
    output_all = lax.all_gather(swap_blocks(output_blocks, "h"), CZ, axis=0)
    output_matrix = (
        output_all.reshape(n_c, n_z, n_h, rows, head_cols)
        .transpose(0, 2, 1, 3, 4)
        .reshape(depth, head_cols)
    )

    local_rows = normalize(hidden[0], norm_gain)
    local_rows = regroup(
        local_rows.reshape(tokens * xl * n_c, depth // n_c), n_h, n_z, rows
    )
    row_blocks = local_rows.reshape(tokens, xl, 1, depth).transpose(1, 2, 0, 3)
    row_blocks = jnp.broadcast_to(row_blocks, (xl, n_h, tokens, depth))
    row_blocks = swap_blocks(row_blocks.reshape(xl * n_h, tokens, depth), XLH)
    chunk = n_h * tokens

    partial = jnp.dot(
        row_blocks.reshape(xl * chunk, depth), proj_weight, preferred_element_type=f32
    ).astype(bf16)
    partial = swap_blocks(partial.reshape(xl, chunk, proj_cols), XL)
    projected = jnp.sum(partial.astype(f32), axis=0)

    half = HEAD_DIMENSION // 2
    frequency = rope_base ** (-jnp.arange(half, dtype=f32) * 2.0 / HEAD_DIMENSION)
    local = jnp.arange(chunk)
    stride = n_z * tokens
    positions = (local // tokens) * stride + lax.axis_index("z") * tokens + local % tokens
    angles = positions.astype(f32)[:, None] * frequency[None, :]
    cosine = jnp.concatenate([jnp.cos(angles), jnp.cos(angles)], axis=-1)
    sine = jnp.concatenate([-jnp.sin(angles), jnp.sin(angles)], axis=-1)

    def rotary(values):
        swapped = jnp.concatenate([values[..., half:], values[..., :half]], axis=-1)
        return (values * cosine + swapped * sine).astype(bf16)

    key_rows = rotary(projected[:, head_cols : head_cols + HEAD_DIMENSION])
    value_rows = projected[:, head_cols + HEAD_DIMENSION :].astype(bf16)
    keyval_rows = lax.all_gather(
        jnp.concatenate([key_rows, value_rows], axis=-1), "z", axis=0, tiled=True
    )
    query_rows = jnp.concatenate(
        [
            rotary(projected[:, i * HEAD_DIMENSION : (i + 1) * HEAD_DIMENSION])
            for i in range(heads)
        ],
        axis=0,
    )

    scores = lax.dot_general(
        query_rows,
        keyval_rows[:, :HEAD_DIMENSION],
        (((1,), (1,)), ((), ())),
        preferred_element_type=f32,
    ) / math.sqrt(HEAD_DIMENSION)
    key_at = jnp.arange(n_z * chunk)
    key_at = key_at // tokens % n_h * stride + key_at // chunk * tokens + key_at % tokens
    query_at = jnp.tile(positions, heads)
    allowed = (key_at[None, :] <= query_at[:, None]) & (key_at[None, :] < lengths[0])
    scores = jnp.where(allowed, scores, masked_score)
    exponent = jnp.exp(scores - jnp.max(scores, axis=-1, keepdims=True))
    attention = (exponent / jnp.sum(exponent, axis=-1, keepdims=True)).astype(bf16)
    head_out = jnp.dot(
        attention, keyval_rows[:, HEAD_DIMENSION:], preferred_element_type=f32
    ).astype(bf16)
    head_out = (
        head_out.reshape(heads, chunk, HEAD_DIMENSION)
        .transpose(1, 0, 2)
        .reshape(chunk, head_cols)
    )

    head_all = swap_blocks(jnp.broadcast_to(head_out[None], (xl,) + head_out.shape), XL)
    mixed = lax.dot_general(
        head_all.reshape(xl * chunk, head_cols),
        output_matrix,
        (((1,), (1,)), ((), ())),
        preferred_element_type=f32,
    ).astype(bf16)
    mixed = swap_blocks(mixed.reshape(xl * n_h, tokens, depth), XLH)
    mixed = jnp.sum(mixed.reshape(xl, n_h, tokens, depth).astype(f32), axis=1).astype(bf16)
    return mixed.transpose(1, 0, 2).reshape(1, tokens, width)


def solution(mesh):
    fine = Mesh(mesh.devices.reshape(4, 2, 2, 4, 8), ("x", "l", "c", "h", "z"))
    section, tensor = ("x", "l", "c"), ("h", "z")
    by_row = P(section + tensor, None)
    return jax.shard_map(
        on_device,
        mesh=fine,
        in_specs=(P(section, tensor, None), P(), P(section)) + (by_row,) * 12,
        out_specs=P(section, tensor, None),
        check_vma=False,
    )
```

```python
import math

import jax
import jax.numpy as jnp
from jax import lax
from jax.sharding import Mesh, PartitionSpec as P

XL = ("x", "l")
XLQ = ("x", "l", "q")
Z = ("r", "q")
CZ = ("c", "r", "q")
CR = ("c", "r")
XLH = ("x", "l", "h")
XLQH = ("x", "l", "q", "h")

QUERY_HEADS_LOCAL = 32
KEYVAL_HEADS = 4
HEAD_DIMENSION = 128

learn_rate = 0.015
beta_one = 0.5
beta_two = 0.9
adam_step = 1000.0
adam_eps = 1e-08
decay_rate = 0.1
norm_eps = 1e-06
rope_base = 1000000.0
masked_score = -1e30


def adam_update(current, gradient, moment, second):
    moment_new = beta_one * moment + (1.0 - beta_one) * gradient
    second_new = beta_two * second + (1.0 - beta_two) * gradient * gradient
    corrected = moment_new / (1.0 - beta_one**adam_step)
    denominator = jnp.sqrt(second_new / (1.0 - beta_two**adam_step)) + adam_eps
    return (current - learn_rate * (corrected / denominator + decay_rate * current)).astype(
        jnp.bfloat16
    )


def normalize(hidden, norm_gain):
    values = hidden.astype(jnp.float32)
    factor = lax.rsqrt(jnp.mean(values * values, axis=-1, keepdims=True) + norm_eps)
    return (values * factor * norm_gain).astype(jnp.bfloat16)


def swap_blocks(blocks, axes):
    return lax.all_to_all(blocks, axes, split_axis=0, concat_axis=0, tiled=True)


def regroup(values, n_h, n_r, n_q, unit):
    size = n_h * n_r * n_q * unit
    target = lax.broadcasted_iota(jnp.int32, (size, size), 1)
    at_h = target // unit % n_h
    at_r = target // (unit * n_h) % n_r
    at_q = target // (unit * n_h * n_r)
    source = ((at_h * n_r + at_r) * n_q + at_q) * unit + target % unit
    matrix = (lax.broadcasted_iota(jnp.int32, (size, size), 0) == source).astype(jnp.bfloat16)
    return jnp.dot(values, matrix, preferred_element_type=jnp.float32).astype(jnp.bfloat16)


def on_device(
    hidden,
    norm_gain,
    lengths,
    query_param,
    query_grad,
    query_moment,
    query_second,
    keyval_param,
    keyval_gradient,
    keyval_first_moment,
    keyval_second_moment,
    output_param,
    output_grad,
    output_moment,
    output_second,
):
    bf16, f32 = jnp.bfloat16, jnp.float32
    xl = lax.axis_size(XL)
    n_h, n_c, n_z = lax.axis_size("h"), lax.axis_size("c"), lax.axis_size(Z)
    n_r, n_q = lax.axis_size("r"), lax.axis_size("q")
    tokens, width = hidden.shape[1], hidden.shape[2]
    rows = query_param.shape[0]
    heads = QUERY_HEADS_LOCAL // n_h
    head_cols = heads * HEAD_DIMENSION
    depth = width // xl

    query_weight = adam_update(query_param, query_grad, query_moment, query_second)
    keyval_weight = adam_update(
        keyval_param, keyval_gradient, keyval_first_moment, keyval_second_moment
    )
    output_weight = adam_update(output_param, output_grad, output_moment, output_second)

    def by_group(weight):
        return weight.reshape(rows, n_h, -1).transpose(1, 0, 2)

    weight_blocks = jnp.concatenate(
        [
            by_group(query_weight),
            by_group(keyval_weight[:, : n_h * HEAD_DIMENSION]),
            by_group(keyval_weight[:, n_h * HEAD_DIMENSION :]),
            by_group(output_weight),
        ],
        axis=2,
    )
    weight_blocks = swap_blocks(weight_blocks, "h")
    proj_cols = head_cols + 2 * HEAD_DIMENSION
    proj_all = lax.all_gather(weight_blocks[:, :, :proj_cols], CR, axis=0)
    proj_weight = proj_all.reshape(depth // n_q, proj_cols)
    output_all = lax.all_gather(weight_blocks[:, :, proj_cols:], CZ, axis=0)
    output_matrix = (
        output_all.reshape(n_c, n_z, n_h, rows, head_cols)
        .transpose(0, 2, 1, 3, 4)
        .reshape(depth, head_cols)
    )

    local_rows = normalize(hidden[0], norm_gain)
    local_rows = regroup(
        local_rows.reshape(tokens * xl * n_c, depth // n_c), n_h, n_r, n_q, rows
    )
    part = depth // n_q
    row_blocks = local_rows.reshape(tokens, xl, n_c, n_q, 1, part // n_c)
    row_blocks = row_blocks.transpose(1, 3, 4, 0, 2, 5).reshape(xl, n_q, 1, tokens, part)
    row_blocks = jnp.broadcast_to(row_blocks, (xl, n_q, n_h, tokens, part))
    row_blocks = swap_blocks(row_blocks.reshape(xl * n_q * n_h, tokens, part), XLQH)
    chunk = n_h * tokens

    partial = jnp.dot(
        row_blocks.reshape(xl * n_q * chunk, part), proj_weight, preferred_element_type=f32
    ).astype(bf16)
    partial = swap_blocks(partial.reshape(xl * n_q, chunk, proj_cols), XLQ)
    projected = jnp.sum(partial.astype(f32), axis=0)

    half = HEAD_DIMENSION // 2
    frequency = rope_base ** (-jnp.arange(half, dtype=f32) * 2.0 / HEAD_DIMENSION)
    local = jnp.arange(chunk)
    stride = n_z * tokens
    positions = (local // tokens) * stride + lax.axis_index(Z) * tokens + local % tokens
    angles = positions.astype(f32)[:, None] * frequency[None, :]
    cosine = jnp.concatenate([jnp.cos(angles), jnp.cos(angles)], axis=-1)
    sine = jnp.concatenate([-jnp.sin(angles), jnp.sin(angles)], axis=-1)

    def rotary(values):
        swapped = jnp.concatenate([values[..., half:], values[..., :half]], axis=-1)
        return (values * cosine + swapped * sine).astype(bf16)

    key_rows = rotary(projected[:, head_cols : head_cols + HEAD_DIMENSION])
    value_rows = projected[:, head_cols + HEAD_DIMENSION :].astype(bf16)
    keyval_rows = jnp.concatenate([key_rows, value_rows], axis=-1)
    keyval_rows = swap_blocks(jnp.broadcast_to(keyval_rows, (n_z,) + keyval_rows.shape), Z)
    keyval_rows = keyval_rows.reshape(n_z * chunk, 2 * HEAD_DIMENSION)
    query_rows = jnp.concatenate(
        [
            rotary(projected[:, i * HEAD_DIMENSION : (i + 1) * HEAD_DIMENSION])
            for i in range(heads)
        ],
        axis=0,
    )

    scores = lax.dot_general(
        query_rows,
        keyval_rows[:, :HEAD_DIMENSION],
        (((1,), (1,)), ((), ())),
        preferred_element_type=f32,
    ) / math.sqrt(HEAD_DIMENSION)
    key_at = jnp.arange(n_z * chunk)
    key_at = key_at // tokens % n_h * stride + key_at // chunk * tokens + key_at % tokens
    query_at = jnp.tile(positions, heads)
    allowed = (key_at[None, :] <= query_at[:, None]) & (key_at[None, :] < lengths[0])
    scores = jnp.where(allowed, scores, masked_score)
    exponent = jnp.exp(scores - jnp.max(scores, axis=-1, keepdims=True))
    attention = (exponent / jnp.sum(exponent, axis=-1, keepdims=True)).astype(bf16)
    head_out = jnp.dot(
        attention, keyval_rows[:, HEAD_DIMENSION:], preferred_element_type=f32
    ).astype(bf16)
    head_out = (
        head_out.reshape(heads, chunk, HEAD_DIMENSION)
        .transpose(1, 0, 2)
        .reshape(chunk, head_cols)
    )

    head_all = swap_blocks(jnp.broadcast_to(head_out[None], (xl,) + head_out.shape), XL)
    mixed = lax.dot_general(
        head_all.reshape(xl * chunk, head_cols),
        output_matrix,
        (((1,), (1,)), ((), ())),
        preferred_element_type=f32,
    ).astype(bf16)
    mixed = swap_blocks(mixed.reshape(xl * n_h, tokens, depth), XLH)
    mixed = jnp.sum(mixed.reshape(xl, n_h, tokens, depth).astype(f32), axis=1).astype(bf16)
    return mixed.transpose(1, 0, 2).reshape(1, tokens, width)


def solution(mesh):
    fine = Mesh(mesh.devices.reshape(4, 2, 2, 4, 4, 2), ("x", "l", "c", "h", "r", "q"))
    section, tensor = ("x", "l", "c"), ("h", "r", "q")
    by_row = P(section + tensor, None)
    return jax.shard_map(
        on_device,
        mesh=fine,
        in_specs=(P(section, tensor, None), P(), P(section)) + (by_row,) * 12,
        out_specs=P(section, tensor, None),
        check_vma=False,
    )
```

```python
import math

import jax
import jax.numpy as jnp
from jax import lax
from jax.sharding import Mesh, PartitionSpec as P

XL = ("x", "l")
CZ = ("c", "z")
XLH = ("x", "l", "h")

QUERY_HEADS_LOCAL = 32
KEYVAL_HEADS = 4
HEAD_DIMENSION = 128

learn_rate = 0.015
beta_one = 0.5
beta_two = 0.9
adam_step = 1000.0
adam_eps = 1e-08
decay_rate = 0.1
norm_eps = 1e-06
rope_base = 1000000.0
masked_score = -1e30


def adam_update(current, gradient, moment, second):
    moment_new = beta_one * moment + (1.0 - beta_one) * gradient
    second_new = beta_two * second + (1.0 - beta_two) * gradient * gradient
    corrected = moment_new / (1.0 - beta_one**adam_step)
    denominator = jnp.sqrt(second_new / (1.0 - beta_two**adam_step)) + adam_eps
    return (current - learn_rate * (corrected / denominator + decay_rate * current)).astype(
        jnp.bfloat16
    )


def normalize(hidden, norm_gain):
    values = hidden.astype(jnp.float32)
    factor = lax.rsqrt(jnp.mean(values * values, axis=-1, keepdims=True) + norm_eps)
    return (values * factor * norm_gain).astype(jnp.bfloat16)


def swap_blocks(blocks, axes):
    return lax.all_to_all(blocks, axes, split_axis=0, concat_axis=0, tiled=True)


def regroup(values, n_h, n_z, unit):
    size = n_h * n_z * unit
    target = lax.broadcasted_iota(jnp.int32, (size, size), 1)
    source = (
        target // unit % n_h * (n_z * unit) + target // (unit * n_h) * unit + target % unit
    )
    matrix = (lax.broadcasted_iota(jnp.int32, (size, size), 0) == source).astype(jnp.bfloat16)
    return jnp.dot(values, matrix, preferred_element_type=jnp.float32).astype(jnp.bfloat16)


def on_device(
    hidden,
    norm_gain,
    lengths,
    query_param,
    query_grad,
    query_moment,
    query_second,
    keyval_param,
    keyval_gradient,
    keyval_first_moment,
    keyval_second_moment,
    output_param,
    output_grad,
    output_moment,
    output_second,
):
    bf16, f32 = jnp.bfloat16, jnp.float32
    xl = lax.axis_size(XL)
    n_h, n_c, n_z = lax.axis_size("h"), lax.axis_size("c"), lax.axis_size("z")
    tokens, width = hidden.shape[1], hidden.shape[2]
    rows = query_param.shape[0]
    heads = QUERY_HEADS_LOCAL // n_h
    head_cols = heads * HEAD_DIMENSION
    depth = width // xl

    query_weight = adam_update(query_param, query_grad, query_moment, query_second)
    keyval_weight = adam_update(
        keyval_param, keyval_gradient, keyval_first_moment, keyval_second_moment
    )
    proj_blocks = jnp.concatenate(
        [
            query_weight.reshape(rows, n_h, head_cols).transpose(1, 0, 2),
            keyval_weight[:, : n_h * HEAD_DIMENSION]
            .reshape(rows, n_h, HEAD_DIMENSION)
            .transpose(1, 0, 2),
            keyval_weight[:, n_h * HEAD_DIMENSION :]
            .reshape(rows, n_h, HEAD_DIMENSION)
            .transpose(1, 0, 2),
        ],
        axis=2,
    )
    proj_cols = proj_blocks.shape[2]
    proj_all = lax.all_gather(swap_blocks(proj_blocks, "h"), CZ, axis=0)
    proj_weight = proj_all.reshape(depth, proj_cols)
    output_weight = adam_update(output_param, output_grad, output_moment, output_second)
    output_blocks = output_weight.reshape(rows, n_h, head_cols).transpose(1, 0, 2)
    output_all = lax.all_gather(swap_blocks(output_blocks, "h"), CZ, axis=0)
    output_matrix = (
        output_all.reshape(n_c, n_z, n_h, rows, head_cols)
        .transpose(0, 2, 1, 3, 4)
        .reshape(depth, head_cols)
    )

    local_rows = normalize(hidden[0], norm_gain)
    local_rows = regroup(
        local_rows.reshape(tokens * xl * n_c, depth // n_c), n_h, n_z, rows
    )
    row_blocks = local_rows.reshape(tokens, xl, 1, depth).transpose(1, 2, 0, 3)
    row_blocks = jnp.broadcast_to(row_blocks, (xl, n_h, tokens, depth))
    row_blocks = swap_blocks(row_blocks.reshape(xl * n_h, tokens, depth), XLH)
    chunk = n_h * tokens

    partial = jnp.dot(
        row_blocks.reshape(xl * chunk, depth), proj_weight, preferred_element_type=f32
    ).astype(bf16)
    partial = swap_blocks(partial.reshape(xl, chunk, proj_cols), XL)
    projected = jnp.sum(partial.astype(f32), axis=0)

    half = HEAD_DIMENSION // 2
    frequency = rope_base ** (-jnp.arange(half, dtype=f32) * 2.0 / HEAD_DIMENSION)
    local = jnp.arange(chunk)
    stride = n_z * tokens
    positions = (local // tokens) * stride + lax.axis_index("z") * tokens + local % tokens
    angles = positions.astype(f32)[:, None] * frequency[None, :]
    cosine = jnp.concatenate([jnp.cos(angles), jnp.cos(angles)], axis=-1)
    sine = jnp.concatenate([-jnp.sin(angles), jnp.sin(angles)], axis=-1)

    def rotary(values):
        swapped = jnp.concatenate([values[..., half:], values[..., :half]], axis=-1)
        return (values * cosine + swapped * sine).astype(bf16)

    key_rows = rotary(projected[:, head_cols : head_cols + HEAD_DIMENSION])
    value_rows = projected[:, head_cols + HEAD_DIMENSION :].astype(bf16)
    keyval_rows = jnp.concatenate([key_rows, value_rows], axis=-1)
    keyval_rows = swap_blocks(jnp.broadcast_to(keyval_rows, (n_z,) + keyval_rows.shape), "z")
    keyval_rows = keyval_rows.reshape(n_z * chunk, 2 * HEAD_DIMENSION)
    query_rows = jnp.concatenate(
        [
            rotary(projected[:, i * HEAD_DIMENSION : (i + 1) * HEAD_DIMENSION])
            for i in range(heads)
        ],
        axis=0,
    )

    scores = lax.dot_general(
        query_rows,
        keyval_rows[:, :HEAD_DIMENSION],
        (((1,), (1,)), ((), ())),
        preferred_element_type=f32,
    ) / math.sqrt(HEAD_DIMENSION)
    key_at = jnp.arange(n_z * chunk)
    key_at = key_at // tokens % n_h * stride + key_at // chunk * tokens + key_at % tokens
    query_at = jnp.tile(positions, heads)
    allowed = (key_at[None, :] <= query_at[:, None]) & (key_at[None, :] < lengths[0])
    scores = jnp.where(allowed, scores, masked_score)
    exponent = jnp.exp(scores - jnp.max(scores, axis=-1, keepdims=True))
    attention = (exponent / jnp.sum(exponent, axis=-1, keepdims=True)).astype(bf16)
    head_out = jnp.dot(
        attention, keyval_rows[:, HEAD_DIMENSION:], preferred_element_type=f32
    ).astype(bf16)
    head_out = (
        head_out.reshape(heads, chunk, HEAD_DIMENSION)
        .transpose(1, 0, 2)
        .reshape(chunk, head_cols)
    )

    head_all = swap_blocks(jnp.broadcast_to(head_out[None], (xl,) + head_out.shape), XL)
    mixed = lax.dot_general(
        head_all.reshape(xl * chunk, head_cols),
        output_matrix,
        (((1,), (1,)), ((), ())),
        preferred_element_type=f32,
    ).astype(bf16)
    mixed = swap_blocks(mixed.reshape(xl * n_h, tokens, depth), XLH)
    mixed = jnp.sum(mixed.reshape(xl, n_h, tokens, depth).astype(f32), axis=1).astype(bf16)
    return mixed.transpose(1, 0, 2).reshape(1, tokens, width)


def solution(mesh):
    fine = Mesh(mesh.devices.reshape(4, 2, 2, 4, 8), ("x", "l", "c", "h", "z"))
    section, tensor = ("x", "l", "c"), ("h", "z")
    by_row = P(section + tensor, None)
    return jax.shard_map(
        on_device,
        mesh=fine,
        in_specs=(P(section, tensor, None), P(), P(section)) + (by_row,) * 12,
        out_specs=P(section, tensor, None),
        check_vma=False,
    )
```

```python
import functools
import math

import jax
import jax.numpy as jnp
from jax import lax
from jax.experimental import pallas as pl
from jax.experimental.pallas import tpu as pltpu
from jax.sharding import Mesh, PartitionSpec as P

XL = ("x", "l")
CZ = ("c", "z")
XLH = ("x", "l", "h")

QUERY_HEADS_LOCAL = 32
KEYVAL_HEADS = 4
HEAD_DIMENSION = 128

learn_rate = 0.015
beta_one = 0.5
beta_two = 0.9
adam_step = 1000.0
adam_eps = 1e-08
decay_rate = 0.1
norm_eps = 1e-06
rope_base = 1000000.0
masked_score = -1e30


unbias_one = 1.0 / (1.0 - beta_one**adam_step)
unbias_two = 1.0 / (1.0 - beta_two**adam_step)


def adam_update(current, gradient, moment, second):
    moment_new = beta_one * moment + (1.0 - beta_one) * gradient
    second_new = beta_two * second + (1.0 - beta_two) * gradient * gradient
    corrected = moment_new * unbias_one
    denominator = jnp.sqrt(second_new * unbias_two) + adam_eps
    return (current - learn_rate * (corrected / denominator + decay_rate * current)).astype(
        jnp.bfloat16
    )


def update_kernel(widths, groups, *refs):
    out_ref = refs[-1]
    for j in range(groups):
        at = 0
        for n, width in enumerate(widths):
            part = [ref[:, j * width : (j + 1) * width] for ref in refs[4 * n : 4 * n + 4]]
            out_ref[j, :, at : at + width] = adam_update(*part)
            at += width


def updated_blocks(parts, n_groups, per_step):
    rows = parts[0][0][0].shape[0]
    widths = [columns // n_groups for _, _, columns in parts]
    specs, arrays = [], []
    for (four, offset, columns), width in zip(parts, widths):
        block = width * per_step
        index = functools.partial(lambda first, i: (0, first + i), offset // block)
        specs += [pl.BlockSpec((rows, block), index)] * 4
        arrays += four
    return pl.pallas_call(
        functools.partial(update_kernel, widths, per_step),
        out_shape=jax.ShapeDtypeStruct((n_groups, rows, sum(widths)), jnp.bfloat16),
        grid=(n_groups // per_step,),
        in_specs=specs,
        out_specs=pl.BlockSpec((per_step, rows, sum(widths)), lambda i: (i, 0, 0)),
        name="update",
    )(*arrays)


def product_kernel(left_ref, right_ref, out_ref):
    out_ref[...] = jnp.dot(
        left_ref[...], right_ref[...], preferred_element_type=jnp.float32
    ).astype(out_ref.dtype)


def product(left, right, block):
    size, depth = left.shape
    columns = right.shape[1]
    return pl.pallas_call(
        product_kernel,
        out_shape=jax.ShapeDtypeStruct((size, columns), jnp.bfloat16),
        grid=(columns // block,),
        in_specs=[
            pl.BlockSpec((size, depth), lambda i: (0, 0)),
            pl.BlockSpec((depth, block), lambda i: (0, i)),
        ],
        out_specs=pl.BlockSpec((size, block), lambda i: (0, i)),
        name="product",
    )(left, right)


def normalize(hidden, norm_gain):
    values = hidden.astype(jnp.float32)
    factor = lax.rsqrt(jnp.mean(values * values, axis=-1, keepdims=True) + norm_eps)
    return (values * factor * norm_gain).astype(jnp.bfloat16)


def swap_blocks(blocks, axes):
    return lax.all_to_all(blocks, axes, split_axis=0, concat_axis=0, tiled=True)


def regroup(values, outer, inner, unit):
    size = outer * inner * unit
    target = lax.broadcasted_iota(jnp.int32, (size, size), 1)
    source = (
        target // unit % outer * (inner * unit)
        + target // (unit * outer) * unit
        + target % unit
    )
    matrix = (lax.broadcasted_iota(jnp.int32, (size, size), 0) == source).astype(jnp.bfloat16)
    return jnp.dot(values, matrix, preferred_element_type=jnp.float32).astype(jnp.bfloat16)


def on_device(
    hidden,
    norm_gain,
    lengths,
    query_param,
    query_grad,
    query_moment,
    query_second,
    keyval_param,
    keyval_gradient,
    keyval_first_moment,
    keyval_second_moment,
    output_param,
    output_grad,
    output_moment,
    output_second,
):
    bf16, f32 = jnp.bfloat16, jnp.float32
    xl = lax.axis_size(XL)
    n_h, n_c, n_z = lax.axis_size("h"), lax.axis_size("c"), lax.axis_size("z")
    tokens, width = hidden.shape[1], hidden.shape[2]
    rows = query_param.shape[0]
    heads = QUERY_HEADS_LOCAL // n_h
    head_cols = heads * HEAD_DIMENSION
    depth = width // xl

    query = [query_param, query_grad, query_moment, query_second]
    keyval = [keyval_param, keyval_gradient, keyval_first_moment, keyval_second_moment]
    output = [output_param, output_grad, output_moment, output_second]
    query_cols = n_h * head_cols
    key_cols = n_h * HEAD_DIMENSION
    proj_blocks = updated_blocks(
        [(query, 0, query_cols), (keyval, 0, key_cols), (keyval, key_cols, key_cols)], n_h, 2
    )
    proj_cols = proj_blocks.shape[2]
    proj_all = lax.all_gather(swap_blocks(proj_blocks, "h"), CZ, axis=0)
    proj_weight = proj_all.reshape(depth, proj_cols)
    output_blocks = updated_blocks([(output, 0, query_cols)], n_h, 2)
    output_all = lax.all_gather(swap_blocks(output_blocks, "h"), CZ, axis=0)
    output_matrix = output_all.reshape(depth, head_cols)

    local_rows = normalize(hidden[0], norm_gain)
    local_rows = regroup(
        local_rows.reshape(tokens * xl * n_c, depth // n_c), n_h, n_z, rows
    )
    row_blocks = local_rows.reshape(tokens, xl, 1, depth).transpose(1, 2, 0, 3)
    row_blocks = jnp.broadcast_to(row_blocks, (xl, n_h, tokens, depth))
    row_blocks = swap_blocks(row_blocks.reshape(xl * n_h, tokens, depth), XLH)
    chunk = n_h * tokens

    partial = product(row_blocks.reshape(xl * chunk, depth), proj_weight, proj_cols // 5)
    partial = swap_blocks(partial.reshape(xl, chunk, proj_cols), XL)
    projected = jnp.sum(partial.astype(f32), axis=0)

    half = HEAD_DIMENSION // 2
    frequency = rope_base ** (-jnp.arange(half, dtype=f32) * 2.0 / HEAD_DIMENSION)
    local = jnp.arange(chunk)
    stride = n_z * tokens
    positions = (local // tokens) * stride + lax.axis_index("z") * tokens + local % tokens
    angles = positions.astype(f32)[:, None] * frequency[None, :]
    cosine = jnp.concatenate([jnp.cos(angles), jnp.cos(angles)], axis=-1)
    sine = jnp.concatenate([-jnp.sin(angles), jnp.sin(angles)], axis=-1)

    def rotary(values):
        swapped = jnp.concatenate([values[..., half:], values[..., :half]], axis=-1)
        return (values * cosine + swapped * sine).astype(bf16)

    key_rows = rotary(projected[:, head_cols : head_cols + HEAD_DIMENSION])
    value_rows = projected[:, head_cols + HEAD_DIMENSION :].astype(bf16)
    keyval_rows = jnp.concatenate([key_rows, value_rows], axis=-1)
    keyval_rows = swap_blocks(jnp.broadcast_to(keyval_rows, (n_z,) + keyval_rows.shape), "z")
    keyval_rows = keyval_rows.reshape(n_z * chunk, 2 * HEAD_DIMENSION)
    query_rows = jnp.concatenate(
        [
            rotary(projected[:, i * HEAD_DIMENSION : (i + 1) * HEAD_DIMENSION])
            for i in range(heads)
        ],
        axis=0,
    )

    scores = lax.dot_general(
        query_rows,
        keyval_rows[:, :HEAD_DIMENSION],
        (((1,), (1,)), ((), ())),
        preferred_element_type=f32,
    ) / math.sqrt(HEAD_DIMENSION)
    key_at = jnp.arange(n_z * chunk)
    key_at = key_at // tokens % n_h * stride + key_at // chunk * tokens + key_at % tokens
    query_at = jnp.tile(positions, heads)
    allowed = (key_at[None, :] <= query_at[:, None]) & (key_at[None, :] < lengths[0])
    scores = jnp.where(allowed, scores, masked_score)
    exponent = jnp.exp(scores - jnp.max(scores, axis=-1, keepdims=True))
    attention = (exponent / jnp.sum(exponent, axis=-1, keepdims=True)).astype(bf16)
    head_out = jnp.dot(
        attention, keyval_rows[:, HEAD_DIMENSION:], preferred_element_type=f32
    ).astype(bf16)
    head_out = (
        head_out.reshape(heads, chunk, HEAD_DIMENSION)
        .transpose(1, 0, 2)
        .reshape(chunk, head_cols)
    )

    head_all = swap_blocks(jnp.broadcast_to(head_out[None], (xl,) + head_out.shape), XL)
    mixed = lax.dot_general(
        head_all.reshape(xl * chunk, head_cols),
        output_matrix,
        (((1,), (1,)), ((), ())),
        preferred_element_type=f32,
    ).astype(bf16)
    mixed = swap_blocks(mixed.reshape(xl * n_h, tokens, depth), XLH)
    mixed = jnp.sum(mixed.reshape(xl, n_h, tokens, depth).astype(f32), axis=1).astype(bf16)
    mixed = regroup(mixed.reshape(xl * tokens * n_c, depth // n_c), n_z, n_h, rows)
    return mixed.reshape(xl, tokens, depth).transpose(1, 0, 2).reshape(1, tokens, width)


def solution(mesh):
    fine = Mesh(mesh.devices.reshape(4, 2, 2, 4, 8), ("x", "l", "c", "h", "z"))
    section, tensor = ("x", "l", "c"), ("h", "z")
    by_row = P(section + tensor, None)
    return jax.shard_map(
        on_device,
        mesh=fine,
        in_specs=(P(section, tensor, None), P(), P(section)) + (by_row,) * 12,
        out_specs=P(section, tensor, None),
        check_vma=False,
    )
```

```python
import math

import jax
import jax.numpy as jnp
from jax import lax
from jax.sharding import Mesh, PartitionSpec as P

XL = ("x", "l")
CZ = ("c", "z")
XLH = ("x", "l", "h")

QUERY_HEADS_LOCAL = 32
KEYVAL_HEADS = 4
HEAD_DIMENSION = 128

learn_rate = 0.015
beta_one = 0.5
beta_two = 0.9
adam_step = 1000.0
adam_eps = 1e-08
decay_rate = 0.1
norm_eps = 1e-06
rope_base = 1000000.0
masked_score = -1e30


def adam_update(current, gradient, moment, second):
    moment_new = beta_one * moment + (1.0 - beta_one) * gradient
    second_new = beta_two * second + (1.0 - beta_two) * gradient * gradient
    corrected = moment_new / (1.0 - beta_one**adam_step)
    denominator = jnp.sqrt(second_new / (1.0 - beta_two**adam_step)) + adam_eps
    return (current - learn_rate * (corrected / denominator + decay_rate * current)).astype(
        jnp.bfloat16
    )


def normalize(hidden, norm_gain):
    values = hidden.astype(jnp.float32)
    factor = lax.rsqrt(jnp.mean(values * values, axis=-1, keepdims=True) + norm_eps)
    return (values * factor * norm_gain).astype(jnp.bfloat16)


def swap_blocks(blocks, axes):
    return lax.all_to_all(blocks, axes, split_axis=0, concat_axis=0, tiled=True)


def regroup(values, n_h, n_z, unit):
    size = n_h * n_z * unit
    target = lax.broadcasted_iota(jnp.int32, (size, size), 1)
    source = (
        target // unit % n_h * (n_z * unit) + target // (unit * n_h) * unit + target % unit
    )
    matrix = (lax.broadcasted_iota(jnp.int32, (size, size), 0) == source).astype(jnp.bfloat16)
    return jnp.dot(values, matrix, preferred_element_type=jnp.float32).astype(jnp.bfloat16)


def on_device(
    hidden,
    norm_gain,
    lengths,
    query_param,
    query_grad,
    query_moment,
    query_second,
    keyval_param,
    keyval_gradient,
    keyval_first_moment,
    keyval_second_moment,
    output_param,
    output_grad,
    output_moment,
    output_second,
):
    bf16, f32 = jnp.bfloat16, jnp.float32
    xl = lax.axis_size(XL)
    n_h, n_c, n_z = lax.axis_size("h"), lax.axis_size("c"), lax.axis_size("z")
    tokens, width = hidden.shape[1], hidden.shape[2]
    rows = query_param.shape[0]
    heads = QUERY_HEADS_LOCAL // n_h
    head_cols = heads * HEAD_DIMENSION
    depth = width // xl

    query_weight = adam_update(query_param, query_grad, query_moment, query_second)
    keyval_weight = adam_update(
        keyval_param, keyval_gradient, keyval_first_moment, keyval_second_moment
    )
    proj_blocks = jnp.concatenate(
        [
            query_weight.reshape(rows, n_h, head_cols).transpose(1, 0, 2),
            keyval_weight[:, : n_h * HEAD_DIMENSION]
            .reshape(rows, n_h, HEAD_DIMENSION)
            .transpose(1, 0, 2),
            keyval_weight[:, n_h * HEAD_DIMENSION :]
            .reshape(rows, n_h, HEAD_DIMENSION)
            .transpose(1, 0, 2),
        ],
        axis=2,
    )
    proj_cols = proj_blocks.shape[2]
    proj_all = lax.all_gather(swap_blocks(proj_blocks, "h"), CZ, axis=0)
    proj_weight = proj_all.reshape(depth, proj_cols)
    output_weight = adam_update(output_param, output_grad, output_moment, output_second)
    output_blocks = output_weight.reshape(rows, n_h, head_cols).transpose(1, 0, 2)
    output_all = lax.all_gather(swap_blocks(output_blocks, "h"), CZ, axis=0)
    output_matrix = (
        output_all.reshape(n_c, n_z, n_h, rows, head_cols)
        .transpose(0, 2, 1, 3, 4)
        .reshape(depth, head_cols)
    )

    chunk = n_h * tokens
    half = HEAD_DIMENSION // 2
    frequency = rope_base ** (-jnp.arange(half, dtype=f32) * 2.0 / HEAD_DIMENSION)
    local = jnp.arange(chunk)
    stride = n_z * tokens
    positions = (local // tokens) * stride + lax.axis_index("z") * tokens + local % tokens
    angles = positions.astype(f32)[:, None] * frequency[None, :]
    cosine = jnp.concatenate([jnp.cos(angles), jnp.cos(angles)], axis=-1)
    sine = jnp.concatenate([-jnp.sin(angles), jnp.sin(angles)], axis=-1)

    key_at = jnp.arange(n_z * chunk)
    key_at = key_at // tokens % n_h * stride + key_at // chunk * tokens + key_at % tokens
    query_at = jnp.tile(positions, heads)
    allowed = (key_at[None, :] <= query_at[:, None]) & (key_at[None, :] < lengths[0])
    local_rows = normalize(hidden[0], norm_gain)
    local_rows, cosine, sine, allowed = lax.optimization_barrier(
        (local_rows, cosine, sine, allowed)
    )
    local_rows = regroup(
        local_rows.reshape(tokens * xl * n_c, depth // n_c), n_h, n_z, rows
    )
    row_blocks = local_rows.reshape(tokens, xl, 1, depth).transpose(1, 2, 0, 3)
    row_blocks = jnp.broadcast_to(row_blocks, (xl, n_h, tokens, depth))
    row_blocks = swap_blocks(row_blocks.reshape(xl * n_h, tokens, depth), XLH)

    partial = jnp.dot(
        row_blocks.reshape(xl * chunk, depth), proj_weight, preferred_element_type=f32
    ).astype(bf16)
    partial = swap_blocks(partial.reshape(xl, chunk, proj_cols), XL)
    query_part = jnp.sum(partial[:, :, :head_cols].astype(f32), axis=0)
    keyval_part = jnp.sum(partial[:, :, head_cols:].astype(f32), axis=0)

    def rotary(values):
        swapped = jnp.concatenate([values[..., half:], values[..., :half]], axis=-1)
        return (values * cosine + swapped * sine).astype(bf16)

    key_rows = rotary(keyval_part[:, :HEAD_DIMENSION])
    value_rows = keyval_part[:, HEAD_DIMENSION:].astype(bf16)
    keyval_rows = jnp.concatenate([key_rows, value_rows], axis=-1)
    keyval_rows = swap_blocks(jnp.broadcast_to(keyval_rows, (n_z,) + keyval_rows.shape), "z")
    keyval_rows = keyval_rows.reshape(n_z * chunk, 2 * HEAD_DIMENSION)
    query_rows = jnp.concatenate(
        [
            rotary(query_part[:, i * HEAD_DIMENSION : (i + 1) * HEAD_DIMENSION])
            for i in range(heads)
        ],
        axis=0,
    )

    scores = lax.dot_general(
        query_rows,
        keyval_rows[:, :HEAD_DIMENSION],
        (((1,), (1,)), ((), ())),
        preferred_element_type=f32,
    ) / math.sqrt(HEAD_DIMENSION)
    scores = jnp.where(allowed, scores, masked_score)
    exponent = jnp.exp(scores - jnp.max(scores, axis=-1, keepdims=True))
    attention = (exponent / jnp.sum(exponent, axis=-1, keepdims=True)).astype(bf16)
    head_out = jnp.dot(
        attention, keyval_rows[:, HEAD_DIMENSION:], preferred_element_type=f32
    ).astype(bf16)
    head_out = (
        head_out.reshape(heads, chunk, HEAD_DIMENSION)
        .transpose(1, 0, 2)
        .reshape(chunk, head_cols)
    )

    head_all = swap_blocks(jnp.broadcast_to(head_out[None], (xl,) + head_out.shape), XL)
    mixed = lax.dot_general(
        head_all.reshape(xl * chunk, head_cols),
        output_matrix,
        (((1,), (1,)), ((), ())),
        preferred_element_type=f32,
    ).astype(bf16)
    mixed = swap_blocks(mixed.reshape(xl * n_h, tokens, depth), XLH)
    mixed = jnp.sum(mixed.reshape(xl, n_h, tokens, depth).astype(f32), axis=1).astype(bf16)
    return mixed.transpose(1, 0, 2).reshape(1, tokens, width)


def solution(mesh):
    fine = Mesh(mesh.devices.reshape(4, 2, 2, 4, 8), ("x", "l", "c", "h", "z"))
    section, tensor = ("x", "l", "c"), ("h", "z")
    by_row = P(section + tensor, None)
    return jax.shard_map(
        on_device,
        mesh=fine,
        in_specs=(P(section, tensor, None), P(), P(section)) + (by_row,) * 12,
        out_specs=P(section, tensor, None),
        check_vma=False,
    )
```

```python
import math

import jax
import jax.numpy as jnp
from jax import lax
from jax.sharding import Mesh, PartitionSpec as P

XL = ("x", "l")
CZ = ("c", "z")
XLH = ("x", "l", "h")

QUERY_HEADS_LOCAL = 32
KEYVAL_HEADS = 4
HEAD_DIMENSION = 128

learn_rate = 0.015
beta_one = 0.5
beta_two = 0.9
adam_step = 1000.0
adam_eps = 1e-08
decay_rate = 0.1
norm_eps = 1e-06
rope_base = 1000000.0
masked_score = -1e30


def adam_update(current, gradient, moment, second):
    moment_new = beta_one * moment + (1.0 - beta_one) * gradient
    second_new = beta_two * second + (1.0 - beta_two) * gradient * gradient
    corrected = moment_new / (1.0 - beta_one**adam_step)
    denominator = jnp.sqrt(second_new / (1.0 - beta_two**adam_step)) + adam_eps
    return (current - learn_rate * (corrected / denominator + decay_rate * current)).astype(
        jnp.bfloat16
    )


def normalize(hidden, norm_gain):
    values = hidden.astype(jnp.float32)
    factor = lax.rsqrt(jnp.mean(values * values, axis=-1, keepdims=True) + norm_eps)
    return (values * factor * norm_gain).astype(jnp.bfloat16)


def swap_blocks(blocks, axes):
    return lax.all_to_all(blocks, axes, split_axis=0, concat_axis=0, tiled=True)


def regroup(values, n_h, n_z, unit):
    size = n_h * n_z * unit
    target = lax.broadcasted_iota(jnp.int32, (size, size), 1)
    source = (
        target // unit % n_h * (n_z * unit) + target // (unit * n_h) * unit + target % unit
    )
    matrix = (lax.broadcasted_iota(jnp.int32, (size, size), 0) == source).astype(jnp.bfloat16)
    return jnp.dot(values, matrix, preferred_element_type=jnp.float32).astype(jnp.bfloat16)


def on_device(
    hidden,
    norm_gain,
    lengths,
    query_param,
    query_grad,
    query_moment,
    query_second,
    keyval_param,
    keyval_gradient,
    keyval_first_moment,
    keyval_second_moment,
    output_param,
    output_grad,
    output_moment,
    output_second,
):
    bf16, f32 = jnp.bfloat16, jnp.float32
    xl = lax.axis_size(XL)
    n_h, n_c, n_z = lax.axis_size("h"), lax.axis_size("c"), lax.axis_size("z")
    tokens, width = hidden.shape[1], hidden.shape[2]
    rows = query_param.shape[0]
    heads = QUERY_HEADS_LOCAL // n_h
    head_cols = heads * HEAD_DIMENSION
    depth = width // xl

    query_weight = adam_update(query_param, query_grad, query_moment, query_second)
    keyval_weight = adam_update(
        keyval_param, keyval_gradient, keyval_first_moment, keyval_second_moment
    )
    proj_blocks = jnp.concatenate(
        [
            query_weight.reshape(rows, n_h, head_cols).transpose(1, 0, 2),
            keyval_weight[:, : n_h * HEAD_DIMENSION]
            .reshape(rows, n_h, HEAD_DIMENSION)
            .transpose(1, 0, 2),
            keyval_weight[:, n_h * HEAD_DIMENSION :]
            .reshape(rows, n_h, HEAD_DIMENSION)
            .transpose(1, 0, 2),
        ],
        axis=2,
    )
    proj_cols = proj_blocks.shape[2]
    proj_all = lax.all_gather(swap_blocks(proj_blocks, "h"), CZ, axis=0)
    proj_weight = proj_all.reshape(depth, proj_cols)
    output_weight = adam_update(output_param, output_grad, output_moment, output_second)
    output_blocks = output_weight.reshape(rows, n_h, head_cols).transpose(1, 0, 2)
    output_all = lax.all_gather(swap_blocks(output_blocks, "h"), CZ, axis=0)
    output_matrix = (
        output_all.reshape(n_c, n_z, n_h, rows, head_cols)
        .transpose(0, 2, 1, 3, 4)
        .reshape(depth, head_cols)
    )

    chunk = n_h * tokens
    half = HEAD_DIMENSION // 2
    frequency = rope_base ** (-jnp.arange(half, dtype=f32) * 2.0 / HEAD_DIMENSION)
    local = jnp.arange(chunk)
    stride = n_z * tokens
    positions = (local // tokens) * stride + lax.axis_index("z") * tokens + local % tokens
    angles = positions.astype(f32)[:, None] * frequency[None, :]
    cosine = jnp.concatenate([jnp.cos(angles), jnp.cos(angles)], axis=-1)
    sine = jnp.concatenate([-jnp.sin(angles), jnp.sin(angles)], axis=-1)

    key_at = jnp.arange(n_z * chunk)
    key_at = key_at // tokens % n_h * stride + key_at // chunk * tokens + key_at % tokens
    query_at = jnp.tile(positions, heads)
    allowed = (key_at[None, :] <= query_at[:, None]) & (key_at[None, :] < lengths[0])
    local_rows = normalize(hidden[0], norm_gain)
    local_rows, cosine, sine, allowed = lax.optimization_barrier(
        (local_rows, cosine, sine, allowed)
    )
    local_rows = regroup(
        local_rows.reshape(tokens * xl * n_c, depth // n_c), n_h, n_z, rows
    )
    row_blocks = local_rows.reshape(tokens, xl, 1, depth).transpose(1, 2, 0, 3)
    row_blocks = jnp.broadcast_to(row_blocks, (xl, n_h, tokens, depth))
    row_blocks = swap_blocks(row_blocks.reshape(xl * n_h, tokens, depth), XLH)

    partial = jnp.dot(
        row_blocks.reshape(xl * chunk, depth), proj_weight, preferred_element_type=f32
    ).astype(jnp.float16)
    partial = swap_blocks(partial.reshape(xl, chunk, proj_cols), XL)
    query_part = jnp.sum(partial[:, :, :head_cols].astype(f32), axis=0)
    keyval_part = jnp.sum(partial[:, :, head_cols:].astype(f32), axis=0)

    def rotary(values):
        swapped = jnp.concatenate([values[..., half:], values[..., :half]], axis=-1)
        return (values * cosine + swapped * sine).astype(bf16)

    key_rows = rotary(keyval_part[:, :HEAD_DIMENSION])
    value_rows = keyval_part[:, HEAD_DIMENSION:].astype(bf16)
    keyval_rows = jnp.concatenate([key_rows, value_rows], axis=-1)
    keyval_rows = swap_blocks(jnp.broadcast_to(keyval_rows, (n_z,) + keyval_rows.shape), "z")
    keyval_rows = keyval_rows.reshape(n_z * chunk, 2 * HEAD_DIMENSION)
    query_rows = jnp.concatenate(
        [
            rotary(query_part[:, i * HEAD_DIMENSION : (i + 1) * HEAD_DIMENSION])
            for i in range(heads)
        ],
        axis=0,
    )

    scores = lax.dot_general(
        query_rows,
        keyval_rows[:, :HEAD_DIMENSION],
        (((1,), (1,)), ((), ())),
        preferred_element_type=f32,
    ) / math.sqrt(HEAD_DIMENSION)
    scores = jnp.where(allowed, scores, masked_score)
    exponent = jnp.exp(scores - jnp.max(scores, axis=-1, keepdims=True))
    attention = (exponent / jnp.sum(exponent, axis=-1, keepdims=True)).astype(bf16)
    head_out = jnp.dot(
        attention, keyval_rows[:, HEAD_DIMENSION:], preferred_element_type=f32
    ).astype(bf16)
    head_out = (
        head_out.reshape(heads, chunk, HEAD_DIMENSION)
        .transpose(1, 0, 2)
        .reshape(chunk, head_cols)
    )

    head_all = swap_blocks(jnp.broadcast_to(head_out[None], (xl,) + head_out.shape), XL)
    mixed = lax.dot_general(
        head_all.reshape(xl * chunk, head_cols),
        output_matrix,
        (((1,), (1,)), ((), ())),
        preferred_element_type=f32,
    ).astype(bf16)
    mixed = swap_blocks(mixed.reshape(xl * n_h, tokens, depth), XLH)
    mixed = jnp.sum(mixed.reshape(xl, n_h, tokens, depth).astype(f32), axis=1).astype(bf16)
    return mixed.transpose(1, 0, 2).reshape(1, tokens, width)


def solution(mesh):
    fine = Mesh(mesh.devices.reshape(4, 2, 2, 4, 8), ("x", "l", "c", "h", "z"))
    section, tensor = ("x", "l", "c"), ("h", "z")
    by_row = P(section + tensor, None)
    return jax.shard_map(
        on_device,
        mesh=fine,
        in_specs=(P(section, tensor, None), P(), P(section)) + (by_row,) * 12,
        out_specs=P(section, tensor, None),
        check_vma=False,
    )
```

```python
import math

import jax
import jax.numpy as jnp
from jax import lax
from jax.sharding import Mesh, PartitionSpec as P

XL = ("x", "l")
Z = ("r", "q")
CZ = ("c", "r", "q")
CR = ("c", "r")
HQ = ("h", "q")
XLH = ("x", "l", "h")

QUERY_HEADS_LOCAL = 32
KEYVAL_HEADS = 4
HEAD_DIMENSION = 128

learn_rate = 0.015
beta_one = 0.5
beta_two = 0.9
adam_step = 1000.0
adam_eps = 1e-08
decay_rate = 0.1
norm_eps = 1e-06
rope_base = 1000000.0
masked_score = -1e30


def adam_update(current, gradient, moment, second):
    moment_new = beta_one * moment + (1.0 - beta_one) * gradient
    second_new = beta_two * second + (1.0 - beta_two) * gradient * gradient
    corrected = moment_new / (1.0 - beta_one**adam_step)
    denominator = jnp.sqrt(second_new / (1.0 - beta_two**adam_step)) + adam_eps
    return (current - learn_rate * (corrected / denominator + decay_rate * current)).astype(
        jnp.bfloat16
    )


def normalize(hidden, norm_gain):
    values = hidden.astype(jnp.float32)
    factor = lax.rsqrt(jnp.mean(values * values, axis=-1, keepdims=True) + norm_eps)
    return (values * factor * norm_gain).astype(jnp.bfloat16)


def swap_blocks(blocks, axes):
    return lax.all_to_all(blocks, axes, split_axis=0, concat_axis=0, tiled=True)


def regroup(values, n_h, n_z, unit):
    size = n_h * n_z * unit
    target = lax.broadcasted_iota(jnp.int32, (size, size), 1)
    source = (
        target // unit % n_h * (n_z * unit) + target // (unit * n_h) * unit + target % unit
    )
    matrix = (lax.broadcasted_iota(jnp.int32, (size, size), 0) == source).astype(jnp.bfloat16)
    return jnp.dot(values, matrix, preferred_element_type=jnp.float32).astype(jnp.bfloat16)


def on_device(
    hidden,
    norm_gain,
    lengths,
    query_param,
    query_grad,
    query_moment,
    query_second,
    keyval_param,
    keyval_gradient,
    keyval_first_moment,
    keyval_second_moment,
    output_param,
    output_grad,
    output_moment,
    output_second,
):
    bf16, f32 = jnp.bfloat16, jnp.float32
    xl = lax.axis_size(XL)
    n_h, n_c, n_z = lax.axis_size("h"), lax.axis_size("c"), lax.axis_size(Z)
    tokens, width = hidden.shape[1], hidden.shape[2]
    rows = query_param.shape[0]
    heads = QUERY_HEADS_LOCAL // n_h
    head_cols = heads * HEAD_DIMENSION
    depth = width // xl

    query_weight = adam_update(query_param, query_grad, query_moment, query_second)
    keyval_weight = adam_update(
        keyval_param, keyval_gradient, keyval_first_moment, keyval_second_moment
    )
    proj_blocks = jnp.concatenate(
        [
            query_weight.reshape(rows, n_h, head_cols).transpose(1, 0, 2),
            keyval_weight[:, : n_h * HEAD_DIMENSION]
            .reshape(rows, n_h, HEAD_DIMENSION)
            .transpose(1, 0, 2),
            keyval_weight[:, n_h * HEAD_DIMENSION :]
            .reshape(rows, n_h, HEAD_DIMENSION)
            .transpose(1, 0, 2),
        ],
        axis=2,
    )
    proj_cols = proj_blocks.shape[2]
    proj_all = lax.all_gather(swap_blocks(proj_blocks, "h"), CZ, axis=0)
    proj_weight = proj_all.reshape(depth, proj_cols)
    output_weight = adam_update(output_param, output_grad, output_moment, output_second)
    output_blocks = output_weight.reshape(rows, n_h, head_cols).transpose(1, 0, 2)
    n_r, n_q = lax.axis_size("r"), lax.axis_size("q")
    output_blocks = jnp.broadcast_to(
        output_blocks[:, None], (n_h, n_q, rows, head_cols)
    ).reshape(n_h * n_q, rows, head_cols)
    output_all = lax.all_gather(swap_blocks(output_blocks, HQ), CR, axis=0)
    output_matrix = (
        output_all.reshape(n_c, n_r, n_h, n_q, rows, head_cols)
        .transpose(0, 2, 1, 3, 4, 5)
        .reshape(depth, head_cols)
    )

    chunk = n_h * tokens
    half = HEAD_DIMENSION // 2
    frequency = rope_base ** (-jnp.arange(half, dtype=f32) * 2.0 / HEAD_DIMENSION)
    local = jnp.arange(chunk)
    stride = n_z * tokens
    positions = (local // tokens) * stride + lax.axis_index(Z) * tokens + local % tokens
    angles = positions.astype(f32)[:, None] * frequency[None, :]
    cosine = jnp.concatenate([jnp.cos(angles), jnp.cos(angles)], axis=-1)
    sine = jnp.concatenate([-jnp.sin(angles), jnp.sin(angles)], axis=-1)

    key_at = jnp.arange(n_z * chunk)
    key_at = key_at // tokens % n_h * stride + key_at // chunk * tokens + key_at % tokens
    query_at = jnp.tile(positions, heads)
    allowed = (key_at[None, :] <= query_at[:, None]) & (key_at[None, :] < lengths[0])
    local_rows = normalize(hidden[0], norm_gain)
    local_rows, cosine, sine, allowed = lax.optimization_barrier(
        (local_rows, cosine, sine, allowed)
    )
    local_rows = regroup(
        local_rows.reshape(tokens * xl * n_c, depth // n_c), n_h, n_z, rows
    )
    row_blocks = local_rows.reshape(tokens, xl, 1, depth).transpose(1, 2, 0, 3)
    row_blocks = jnp.broadcast_to(row_blocks, (xl, n_h, tokens, depth))
    row_blocks = swap_blocks(row_blocks.reshape(xl * n_h, tokens, depth), XLH)

    partial = jnp.dot(
        row_blocks.reshape(xl * chunk, depth), proj_weight, preferred_element_type=f32
    ).astype(jnp.float16)
    partial = swap_blocks(partial.reshape(xl, chunk, proj_cols), XL)
    query_part = jnp.sum(partial[:, :, :head_cols].astype(f32), axis=0)
    keyval_part = jnp.sum(partial[:, :, head_cols:].astype(f32), axis=0)

    def rotary(values):
        swapped = jnp.concatenate([values[..., half:], values[..., :half]], axis=-1)
        return (values * cosine + swapped * sine).astype(bf16)

    key_rows = rotary(keyval_part[:, :HEAD_DIMENSION])
    value_rows = keyval_part[:, HEAD_DIMENSION:].astype(bf16)
    keyval_rows = jnp.concatenate([key_rows, value_rows], axis=-1)
    keyval_rows = swap_blocks(jnp.broadcast_to(keyval_rows, (n_z,) + keyval_rows.shape), Z)
    keyval_rows = keyval_rows.reshape(n_z * chunk, 2 * HEAD_DIMENSION)
    query_rows = jnp.concatenate(
        [
            rotary(query_part[:, i * HEAD_DIMENSION : (i + 1) * HEAD_DIMENSION])
            for i in range(heads)
        ],
        axis=0,
    )

    scores = lax.dot_general(
        query_rows,
        keyval_rows[:, :HEAD_DIMENSION],
        (((1,), (1,)), ((), ())),
        preferred_element_type=f32,
    ) / math.sqrt(HEAD_DIMENSION)
    scores = jnp.where(allowed, scores, masked_score)
    exponent = jnp.exp(scores - jnp.max(scores, axis=-1, keepdims=True))
    attention = (exponent / jnp.sum(exponent, axis=-1, keepdims=True)).astype(bf16)
    head_out = jnp.dot(
        attention, keyval_rows[:, HEAD_DIMENSION:], preferred_element_type=f32
    ).astype(bf16)
    head_out = (
        head_out.reshape(heads, chunk, HEAD_DIMENSION)
        .transpose(1, 0, 2)
        .reshape(chunk, head_cols)
    )

    head_all = swap_blocks(jnp.broadcast_to(head_out[None], (xl,) + head_out.shape), XL)
    mixed = lax.dot_general(
        head_all.reshape(xl * chunk, head_cols),
        output_matrix,
        (((1,), (1,)), ((), ())),
        preferred_element_type=f32,
    ).astype(bf16)
    mixed = swap_blocks(mixed.reshape(xl * n_h, tokens, depth), XLH)
    mixed = jnp.sum(mixed.reshape(xl, n_h, tokens, depth).astype(f32), axis=1).astype(bf16)
    return mixed.transpose(1, 0, 2).reshape(1, tokens, width)


def solution(mesh):
    fine = Mesh(mesh.devices.reshape(4, 2, 2, 4, 4, 2), ("x", "l", "c", "h", "r", "q"))
    section, tensor = ("x", "l", "c"), ("h", "r", "q")
    by_row = P(section + tensor, None)
    return jax.shard_map(
        on_device,
        mesh=fine,
        in_specs=(P(section, tensor, None), P(), P(section)) + (by_row,) * 12,
        out_specs=P(section, tensor, None),
        check_vma=False,
    )
```

```python
import math

import jax
import jax.numpy as jnp
from jax import lax
from jax.sharding import Mesh, PartitionSpec as P

XL = ("x", "l")
Z = ("r", "q")
CZ = ("c", "r", "q")
CR = ("c", "r")
HQ = ("h", "q")
XLH = ("x", "l", "h")

QUERY_HEADS_LOCAL = 32
KEYVAL_HEADS = 4
HEAD_DIMENSION = 128

learn_rate = 0.015
beta_one = 0.5
beta_two = 0.9
adam_step = 1000.0
adam_eps = 1e-08
decay_rate = 0.1
norm_eps = 1e-06
rope_base = 1000000.0
masked_score = -1e30


def adam_update(current, gradient, moment, second):
    moment_new = beta_one * moment + (1.0 - beta_one) * gradient
    second_new = beta_two * second + (1.0 - beta_two) * gradient * gradient
    corrected = moment_new / (1.0 - beta_one**adam_step)
    denominator = jnp.sqrt(second_new / (1.0 - beta_two**adam_step)) + adam_eps
    return (current - learn_rate * (corrected / denominator + decay_rate * current)).astype(
        jnp.bfloat16
    )


def normalize(hidden, norm_gain):
    values = hidden.astype(jnp.float32)
    factor = lax.rsqrt(jnp.mean(values * values, axis=-1, keepdims=True) + norm_eps)
    return (values * factor * norm_gain).astype(jnp.bfloat16)


def swap_blocks(blocks, axes):
    return lax.all_to_all(blocks, axes, split_axis=0, concat_axis=0, tiled=True)


def regroup(values, n_h, n_z, unit):
    size = n_h * n_z * unit
    target = lax.broadcasted_iota(jnp.int32, (size, size), 1)
    source = (
        target // unit % n_h * (n_z * unit) + target // (unit * n_h) * unit + target % unit
    )
    matrix = (lax.broadcasted_iota(jnp.int32, (size, size), 0) == source).astype(jnp.bfloat16)
    return jnp.dot(values, matrix, preferred_element_type=jnp.float32).astype(jnp.bfloat16)


def on_device(
    hidden,
    norm_gain,
    lengths,
    query_param,
    query_grad,
    query_moment,
    query_second,
    keyval_param,
    keyval_gradient,
    keyval_first_moment,
    keyval_second_moment,
    output_param,
    output_grad,
    output_moment,
    output_second,
):
    bf16, f32 = jnp.bfloat16, jnp.float32
    xl = lax.axis_size(XL)
    n_h, n_c, n_z = lax.axis_size("h"), lax.axis_size("c"), lax.axis_size(Z)
    tokens, width = hidden.shape[1], hidden.shape[2]
    rows = query_param.shape[0]
    heads = QUERY_HEADS_LOCAL // n_h
    head_cols = heads * HEAD_DIMENSION
    depth = width // xl

    query_weight = adam_update(query_param, query_grad, query_moment, query_second)
    keyval_weight = adam_update(
        keyval_param, keyval_gradient, keyval_first_moment, keyval_second_moment
    )
    proj_blocks = jnp.concatenate(
        [
            query_weight.reshape(rows, n_h, head_cols).transpose(1, 0, 2),
            keyval_weight[:, : n_h * HEAD_DIMENSION]
            .reshape(rows, n_h, HEAD_DIMENSION)
            .transpose(1, 0, 2),
            keyval_weight[:, n_h * HEAD_DIMENSION :]
            .reshape(rows, n_h, HEAD_DIMENSION)
            .transpose(1, 0, 2),
        ],
        axis=2,
    )
    proj_cols = proj_blocks.shape[2]
    proj_all = lax.all_gather(swap_blocks(proj_blocks, "h"), CZ, axis=0)
    proj_weight = proj_all.reshape(depth, proj_cols)
    output_weight = adam_update(output_param, output_grad, output_moment, output_second)
    output_blocks = output_weight.reshape(rows, n_h, head_cols).transpose(1, 0, 2)
    n_r, n_q = lax.axis_size("r"), lax.axis_size("q")
    output_blocks = jnp.broadcast_to(
        output_blocks[:, None], (n_h, n_q, rows, head_cols)
    ).reshape(n_h * n_q, rows, head_cols)
    output_all = lax.all_gather(swap_blocks(output_blocks, HQ), CR, axis=0)
    output_matrix = (
        output_all.reshape(n_c, n_r, n_h, n_q, rows, head_cols)
        .transpose(0, 2, 1, 3, 4, 5)
        .reshape(depth, head_cols)
    )

    chunk = n_h * tokens
    half = HEAD_DIMENSION // 2
    frequency = rope_base ** (-jnp.arange(half, dtype=f32) * 2.0 / HEAD_DIMENSION)
    local = jnp.arange(chunk)
    stride = n_z * tokens
    positions = (local // tokens) * stride + lax.axis_index(Z) * tokens + local % tokens
    angles = positions.astype(f32)[:, None] * frequency[None, :]
    cosine = jnp.concatenate([jnp.cos(angles), jnp.cos(angles)], axis=-1)
    sine = jnp.concatenate([-jnp.sin(angles), jnp.sin(angles)], axis=-1)

    key_at = jnp.arange(n_z * chunk)
    key_at = key_at // tokens % n_h * stride + key_at // chunk * tokens + key_at % tokens
    query_at = jnp.tile(positions, heads)
    allowed = (key_at[None, :] <= query_at[:, None]) & (key_at[None, :] < lengths[0])
    local_rows = normalize(hidden[0], norm_gain)
    local_rows, cosine, sine, allowed = lax.optimization_barrier(
        (local_rows, cosine, sine, allowed)
    )
    local_rows = regroup(
        local_rows.reshape(tokens * xl * n_c, depth // n_c), n_h, n_z, rows
    )
    row_blocks = local_rows.reshape(tokens, xl, 1, depth).transpose(1, 2, 0, 3)
    row_blocks = jnp.broadcast_to(row_blocks, (xl, n_h, tokens, depth))
    row_blocks = swap_blocks(row_blocks.reshape(xl * n_h, tokens, depth), XLH)

    partial = jnp.dot(
        row_blocks.reshape(xl * chunk, depth), proj_weight, preferred_element_type=f32
    ).astype(jnp.float16)
    partial = swap_blocks(partial.reshape(xl, chunk, proj_cols), XL)
    query_part = jnp.sum(partial[:, :, :head_cols].astype(f32), axis=0)
    keyval_part = jnp.sum(partial[:, :, head_cols:].astype(f32), axis=0)

    def rotary(values):
        swapped = jnp.concatenate([values[..., half:], values[..., :half]], axis=-1)
        return (values * cosine + swapped * sine).astype(bf16)

    key_rows = rotary(keyval_part[:, :HEAD_DIMENSION])
    value_rows = keyval_part[:, HEAD_DIMENSION:].astype(bf16)
    query_rows = jnp.concatenate(
        [
            rotary(query_part[:, i * HEAD_DIMENSION : (i + 1) * HEAD_DIMENSION])
            for i in range(heads)
        ],
        axis=0,
    )
    keyval_rows = jnp.concatenate([key_rows, value_rows], axis=-1)
    keyval_rows, query_rows = lax.optimization_barrier((keyval_rows, query_rows))
    keyval_rows = swap_blocks(jnp.broadcast_to(keyval_rows, (n_z,) + keyval_rows.shape), Z)
    keyval_rows = keyval_rows.reshape(n_z * chunk, 2 * HEAD_DIMENSION)
    scores = lax.dot_general(
        query_rows,
        keyval_rows[:, :HEAD_DIMENSION],
        (((1,), (1,)), ((), ())),
        preferred_element_type=f32,
    ) / math.sqrt(HEAD_DIMENSION)
    scores = jnp.where(allowed, scores, masked_score)
    exponent = jnp.exp(scores - jnp.max(scores, axis=-1, keepdims=True))
    attention = (exponent / jnp.sum(exponent, axis=-1, keepdims=True)).astype(bf16)
    head_out = jnp.dot(
        attention, keyval_rows[:, HEAD_DIMENSION:], preferred_element_type=f32
    ).astype(bf16)
    head_out = (
        head_out.reshape(heads, chunk, HEAD_DIMENSION)
        .transpose(1, 0, 2)
        .reshape(chunk, head_cols)
    )

    head_all = swap_blocks(jnp.broadcast_to(head_out[None], (xl,) + head_out.shape), XL)
    mixed = lax.dot_general(
        head_all.reshape(xl * chunk, head_cols),
        output_matrix,
        (((1,), (1,)), ((), ())),
        preferred_element_type=f32,
    ).astype(bf16)
    mixed = swap_blocks(mixed.reshape(xl * n_h, tokens, depth), XLH)
    mixed = jnp.sum(mixed.reshape(xl, n_h, tokens, depth).astype(f32), axis=1).astype(bf16)
    return mixed.transpose(1, 0, 2).reshape(1, tokens, width)


def solution(mesh):
    fine = Mesh(mesh.devices.reshape(4, 2, 2, 4, 4, 2), ("x", "l", "c", "h", "r", "q"))
    section, tensor = ("x", "l", "c"), ("h", "r", "q")
    by_row = P(section + tensor, None)
    return jax.shard_map(
        on_device,
        mesh=fine,
        in_specs=(P(section, tensor, None), P(), P(section)) + (by_row,) * 12,
        out_specs=P(section, tensor, None),
        check_vma=False,
    )
```

```python
import math

import jax
import jax.numpy as jnp
from jax import lax
from jax.sharding import Mesh, PartitionSpec as P

XL = ("x", "l")
Z = ("r", "q")
CZ = ("c", "r", "q")
CR = ("c", "r")
HQ = ("h", "q")
XLH = ("x", "l", "h")

QUERY_HEADS_LOCAL = 32
KEYVAL_HEADS = 4
HEAD_DIMENSION = 128

learn_rate = 0.015
beta_one = 0.5
beta_two = 0.9
adam_step = 1000.0
adam_eps = 1e-08
decay_rate = 0.1
norm_eps = 1e-06
rope_base = 1000000.0
masked_score = -1e30


def adam_update(current, gradient, moment, second):
    moment_new = beta_one * moment + (1.0 - beta_one) * gradient
    second_new = beta_two * second + (1.0 - beta_two) * gradient * gradient
    corrected = moment_new / (1.0 - beta_one**adam_step)
    denominator = jnp.sqrt(second_new / (1.0 - beta_two**adam_step)) + adam_eps
    return (current - learn_rate * (corrected / denominator + decay_rate * current)).astype(
        jnp.bfloat16
    )


def normalize(hidden, norm_gain):
    values = hidden.astype(jnp.float32)
    factor = lax.rsqrt(jnp.mean(values * values, axis=-1, keepdims=True) + norm_eps)
    return (values * factor * norm_gain).astype(jnp.bfloat16)


def swap_blocks(blocks, axes):
    return lax.all_to_all(blocks, axes, split_axis=0, concat_axis=0, tiled=True)


def regroup(values, n_h, n_z, unit):
    size = n_h * n_z * unit
    target = lax.broadcasted_iota(jnp.int32, (size, size), 1)
    source = (
        target // unit % n_h * (n_z * unit) + target // (unit * n_h) * unit + target % unit
    )
    matrix = (lax.broadcasted_iota(jnp.int32, (size, size), 0) == source).astype(jnp.bfloat16)
    return jnp.dot(values, matrix, preferred_element_type=jnp.float32).astype(jnp.bfloat16)


def on_device(
    hidden,
    norm_gain,
    lengths,
    query_param,
    query_grad,
    query_moment,
    query_second,
    keyval_param,
    keyval_gradient,
    keyval_first_moment,
    keyval_second_moment,
    output_param,
    output_grad,
    output_moment,
    output_second,
):
    bf16, f32 = jnp.bfloat16, jnp.float32
    xl = lax.axis_size(XL)
    n_h, n_c, n_z = lax.axis_size("h"), lax.axis_size("c"), lax.axis_size(Z)
    tokens, width = hidden.shape[1], hidden.shape[2]
    rows = query_param.shape[0]
    heads = QUERY_HEADS_LOCAL // n_h
    head_cols = heads * HEAD_DIMENSION
    depth = width // xl

    query_weight = adam_update(query_param, query_grad, query_moment, query_second)
    keyval_weight = adam_update(
        keyval_param, keyval_gradient, keyval_first_moment, keyval_second_moment
    )
    proj_blocks = jnp.concatenate(
        [
            query_weight.reshape(rows, n_h, head_cols).transpose(1, 0, 2),
            keyval_weight[:, : n_h * HEAD_DIMENSION]
            .reshape(rows, n_h, HEAD_DIMENSION)
            .transpose(1, 0, 2),
            keyval_weight[:, n_h * HEAD_DIMENSION :]
            .reshape(rows, n_h, HEAD_DIMENSION)
            .transpose(1, 0, 2),
        ],
        axis=2,
    )
    proj_cols = proj_blocks.shape[2]
    proj_all = lax.all_gather(swap_blocks(proj_blocks, "h"), CZ, axis=0)
    proj_weight = proj_all.reshape(depth, proj_cols)
    output_weight = adam_update(output_param, output_grad, output_moment, output_second)
    output_blocks = output_weight.reshape(rows, n_h, head_cols).transpose(1, 0, 2)
    n_r, n_q = lax.axis_size("r"), lax.axis_size("q")
    output_blocks = jnp.broadcast_to(
        output_blocks[:, None], (n_h, n_q, rows, head_cols)
    ).reshape(n_h * n_q, rows, head_cols)
    output_all = lax.all_gather(swap_blocks(output_blocks, HQ), CR, axis=0)
    output_matrix = (
        output_all.reshape(n_c, n_r, n_h, n_q, rows, head_cols)
        .transpose(0, 2, 1, 3, 4, 5)
        .reshape(depth, head_cols)
    )

    chunk = n_h * tokens
    half = HEAD_DIMENSION // 2
    frequency = rope_base ** (-jnp.arange(half, dtype=f32) * 2.0 / HEAD_DIMENSION)
    local = jnp.arange(chunk)
    stride = n_z * tokens
    positions = (local // tokens) * stride + lax.axis_index(Z) * tokens + local % tokens
    angles = positions.astype(f32)[:, None] * frequency[None, :]
    cosine = jnp.concatenate([jnp.cos(angles), jnp.cos(angles)], axis=-1)
    sine = jnp.concatenate([-jnp.sin(angles), jnp.sin(angles)], axis=-1)

    key_at = jnp.arange(n_z * chunk)
    key_at = key_at // tokens % n_h * stride + key_at // chunk * tokens + key_at % tokens
    query_at = jnp.tile(positions, heads)
    allowed = (key_at[None, :] <= query_at[:, None]) & (key_at[None, :] < lengths[0])
    local_rows = normalize(hidden[0], norm_gain)
    local_rows, cosine, sine, allowed = lax.optimization_barrier(
        (local_rows, cosine, sine, allowed)
    )
    local_rows = regroup(
        local_rows.reshape(tokens * xl * n_c, depth // n_c), n_h, n_z, rows
    )
    row_blocks = local_rows.reshape(tokens, xl, 1, depth).transpose(1, 2, 0, 3)
    row_blocks = jnp.broadcast_to(row_blocks, (xl, n_h, tokens, depth))
    row_blocks = swap_blocks(row_blocks.reshape(xl * n_h, tokens, depth), XLH)

    lift = jnp.where(jnp.arange(proj_cols) < head_cols, 1.0, 32.0).astype(f32)
    partial = jnp.dot(
        row_blocks.reshape(xl * chunk, depth), proj_weight, preferred_element_type=f32
    )
    partial = (partial * lift).astype(jnp.float16)
    partial = swap_blocks(partial.reshape(xl, chunk, proj_cols), XL)
    query_part = jnp.sum(partial[:, :, :head_cols].astype(f32), axis=0)
    keyval_part = jnp.sum(partial[:, :, head_cols:].astype(f32), axis=0) * (1.0 / 32.0)

    def rotary(values):
        swapped = jnp.concatenate([values[..., half:], values[..., :half]], axis=-1)
        return (values * cosine + swapped * sine).astype(bf16)

    key_rows = rotary(keyval_part[:, :HEAD_DIMENSION])
    value_rows = keyval_part[:, HEAD_DIMENSION:].astype(bf16)
    query_rows = jnp.concatenate(
        [
            rotary(query_part[:, i * HEAD_DIMENSION : (i + 1) * HEAD_DIMENSION])
            for i in range(heads)
        ],
        axis=0,
    )
    keyval_rows = jnp.concatenate([key_rows, value_rows], axis=-1)
    keyval_rows, query_rows = lax.optimization_barrier((keyval_rows, query_rows))
    keyval_rows = swap_blocks(jnp.broadcast_to(keyval_rows, (n_z,) + keyval_rows.shape), Z)
    keyval_rows = keyval_rows.reshape(n_z * chunk, 2 * HEAD_DIMENSION)
    scores = lax.dot_general(
        query_rows,
        keyval_rows[:, :HEAD_DIMENSION],
        (((1,), (1,)), ((), ())),
        preferred_element_type=f32,
    ) / math.sqrt(HEAD_DIMENSION)
    scores = jnp.where(allowed, scores, masked_score)
    exponent = jnp.exp(scores - jnp.max(scores, axis=-1, keepdims=True))
    attention = (exponent / jnp.sum(exponent, axis=-1, keepdims=True)).astype(bf16)
    head_out = jnp.dot(
        attention, keyval_rows[:, HEAD_DIMENSION:], preferred_element_type=f32
    ).astype(bf16)
    head_out = (
        head_out.reshape(heads, chunk, HEAD_DIMENSION)
        .transpose(1, 0, 2)
        .reshape(chunk, head_cols)
    )

    head_all = swap_blocks(jnp.broadcast_to(head_out[None], (xl,) + head_out.shape), XL)
    mixed = lax.dot_general(
        head_all.reshape(xl * chunk, head_cols),
        output_matrix,
        (((1,), (1,)), ((), ())),
        preferred_element_type=f32,
    ).astype(bf16)
    mixed = swap_blocks(mixed.reshape(xl * n_h, tokens, depth), XLH)
    mixed = jnp.sum(mixed.reshape(xl, n_h, tokens, depth).astype(f32), axis=1).astype(bf16)
    return mixed.transpose(1, 0, 2).reshape(1, tokens, width)


def solution(mesh):
    fine = Mesh(mesh.devices.reshape(4, 2, 2, 4, 4, 2), ("x", "l", "c", "h", "r", "q"))
    section, tensor = ("x", "l", "c"), ("h", "r", "q")
    by_row = P(section + tensor, None)
    return jax.shard_map(
        on_device,
        mesh=fine,
        in_specs=(P(section, tensor, None), P(), P(section)) + (by_row,) * 12,
        out_specs=P(section, tensor, None),
        check_vma=False,
    )
```

```python
import math

import jax
import jax.numpy as jnp
from jax import lax
from jax.sharding import Mesh, PartitionSpec as P

XL = ("x", "l")
Z = ("r", "q")
CZ = ("c", "r", "q")
CR = ("c", "r")
HQ = ("h", "q")
XLH = ("x", "l", "h")

QUERY_HEADS_LOCAL = 32
KEYVAL_HEADS = 4
HEAD_DIMENSION = 128

learn_rate = 0.015
beta_one = 0.5
beta_two = 0.9
adam_step = 1000.0
adam_eps = 1e-08
decay_rate = 0.1
norm_eps = 1e-06
rope_base = 1000000.0
masked_score = -1e30


def adam_update(current, gradient, moment, second):
    moment_new = beta_one * moment + (1.0 - beta_one) * gradient
    second_new = beta_two * second + (1.0 - beta_two) * gradient * gradient
    corrected = moment_new / (1.0 - beta_one**adam_step)
    denominator = jnp.sqrt(second_new / (1.0 - beta_two**adam_step)) + adam_eps
    return (current - learn_rate * (corrected / denominator + decay_rate * current)).astype(
        jnp.bfloat16
    )


def normalize(hidden, norm_gain):
    values = hidden.astype(jnp.float32)
    factor = lax.rsqrt(jnp.mean(values * values, axis=-1, keepdims=True) + norm_eps)
    return (values * factor * norm_gain).astype(jnp.bfloat16)


def swap_blocks(blocks, axes):
    return lax.all_to_all(blocks, axes, split_axis=0, concat_axis=0, tiled=True)


def regroup(values, n_h, n_z, unit):
    size = n_h * n_z * unit
    target = lax.broadcasted_iota(jnp.int32, (size, size), 1)
    source = (
        target // unit % n_h * (n_z * unit) + target // (unit * n_h) * unit + target % unit
    )
    matrix = (lax.broadcasted_iota(jnp.int32, (size, size), 0) == source).astype(jnp.bfloat16)
    return jnp.dot(values, matrix, preferred_element_type=jnp.float32).astype(jnp.bfloat16)


def on_device(
    hidden,
    norm_gain,
    lengths,
    query_param,
    query_grad,
    query_moment,
    query_second,
    keyval_param,
    keyval_gradient,
    keyval_first_moment,
    keyval_second_moment,
    output_param,
    output_grad,
    output_moment,
    output_second,
):
    bf16, f32 = jnp.bfloat16, jnp.float32
    xl = lax.axis_size(XL)
    n_h, n_c, n_z = lax.axis_size("h"), lax.axis_size("c"), lax.axis_size(Z)
    tokens, width = hidden.shape[1], hidden.shape[2]
    rows = query_param.shape[0]
    heads = QUERY_HEADS_LOCAL // n_h
    head_cols = heads * HEAD_DIMENSION
    depth = width // xl

    query_weight = adam_update(query_param, query_grad, query_moment, query_second)
    keyval_weight = adam_update(
        keyval_param, keyval_gradient, keyval_first_moment, keyval_second_moment
    )
    proj_blocks = jnp.concatenate(
        [
            query_weight.reshape(rows, n_h, head_cols).transpose(1, 0, 2),
            keyval_weight[:, : n_h * HEAD_DIMENSION]
            .reshape(rows, n_h, HEAD_DIMENSION)
            .transpose(1, 0, 2),
            keyval_weight[:, n_h * HEAD_DIMENSION :]
            .reshape(rows, n_h, HEAD_DIMENSION)
            .transpose(1, 0, 2),
        ],
        axis=2,
    )
    proj_cols = proj_blocks.shape[2]
    proj_all = lax.all_gather(swap_blocks(proj_blocks, "h"), CZ, axis=0)
    proj_weight = proj_all.reshape(depth, proj_cols)
    output_weight = adam_update(output_param, output_grad, output_moment, output_second)
    output_blocks = output_weight.reshape(rows, n_h, head_cols).transpose(1, 0, 2)
    n_r, n_q = lax.axis_size("r"), lax.axis_size("q")
    output_blocks = jnp.broadcast_to(
        output_blocks[:, None], (n_h, n_q, rows, head_cols)
    ).reshape(n_h * n_q, rows, head_cols)
    output_all = lax.all_gather(swap_blocks(output_blocks, HQ), CR, axis=0)
    output_matrix = (
        output_all.reshape(n_c, n_r, n_h, n_q, rows, head_cols)
        .transpose(0, 2, 1, 3, 4, 5)
        .reshape(depth, head_cols)
    )

    chunk = n_h * tokens
    half = HEAD_DIMENSION // 2
    frequency = rope_base ** (-jnp.arange(half, dtype=f32) * 2.0 / HEAD_DIMENSION)
    local = jnp.arange(chunk)
    stride = n_z * tokens
    positions = (local // tokens) * stride + lax.axis_index(Z) * tokens + local % tokens
    angles = positions.astype(f32)[:, None] * frequency[None, :]
    cosine = jnp.concatenate([jnp.cos(angles), jnp.cos(angles)], axis=-1)
    sine = jnp.concatenate([-jnp.sin(angles), jnp.sin(angles)], axis=-1)

    key_at = jnp.arange(n_z * chunk)
    key_at = key_at // tokens % n_h * stride + key_at // chunk * tokens + key_at % tokens
    query_at = jnp.tile(positions, heads)
    allowed = (key_at[None, :] <= query_at[:, None]) & (key_at[None, :] < lengths[0])
    local_rows = normalize(hidden[0], norm_gain)
    lift = jnp.where(jnp.arange(proj_cols) < head_cols, 1.0, 32.0).astype(f32)
    local_rows, cosine, sine, allowed, lift = lax.optimization_barrier(
        (local_rows, cosine, sine, allowed, lift)
    )
    local_rows = regroup(
        local_rows.reshape(tokens * xl * n_c, depth // n_c), n_h, n_z, rows
    )
    row_blocks = local_rows.reshape(tokens, xl, 1, depth).transpose(1, 2, 0, 3)
    row_blocks = jnp.broadcast_to(row_blocks, (xl, n_h, tokens, depth))
    row_blocks = swap_blocks(row_blocks.reshape(xl * n_h, tokens, depth), XLH)

    partial = jnp.dot(
        row_blocks.reshape(xl * chunk, depth), proj_weight, preferred_element_type=f32
    )
    partial = (partial * lift).astype(jnp.float16)
    partial = swap_blocks(partial.reshape(xl, chunk, proj_cols), XL)
    query_part = jnp.sum(partial[:, :, :head_cols].astype(f32), axis=0)
    keyval_part = jnp.sum(partial[:, :, head_cols:].astype(f32), axis=0) * (1.0 / 32.0)

    def rotary(values):
        swapped = jnp.concatenate([values[..., half:], values[..., :half]], axis=-1)
        return (values * cosine + swapped * sine).astype(bf16)

    key_rows = rotary(keyval_part[:, :HEAD_DIMENSION])
    value_rows = keyval_part[:, HEAD_DIMENSION:].astype(bf16)
    query_rows = jnp.concatenate(
        [
            rotary(query_part[:, i * HEAD_DIMENSION : (i + 1) * HEAD_DIMENSION])
            for i in range(heads)
        ],
        axis=0,
    )
    keyval_rows = jnp.concatenate([key_rows, value_rows], axis=-1)
    keyval_rows, query_rows = lax.optimization_barrier((keyval_rows, query_rows))
    keyval_rows = swap_blocks(jnp.broadcast_to(keyval_rows, (n_z,) + keyval_rows.shape), Z)
    keyval_rows = keyval_rows.reshape(n_z * chunk, 2 * HEAD_DIMENSION)
    scores = lax.dot_general(
        query_rows,
        keyval_rows[:, :HEAD_DIMENSION],
        (((1,), (1,)), ((), ())),
        preferred_element_type=f32,
    ) / math.sqrt(HEAD_DIMENSION)
    scores = jnp.where(allowed, scores, masked_score)
    exponent = jnp.exp(scores - jnp.max(scores, axis=-1, keepdims=True))
    attention = (exponent / jnp.sum(exponent, axis=-1, keepdims=True)).astype(bf16)
    head_out = jnp.dot(
        attention, keyval_rows[:, HEAD_DIMENSION:], preferred_element_type=f32
    ).astype(bf16)
    head_out = (
        head_out.reshape(heads, chunk, HEAD_DIMENSION)
        .transpose(1, 0, 2)
        .reshape(chunk, head_cols)
    )

    head_all = swap_blocks(jnp.broadcast_to(head_out[None], (xl,) + head_out.shape), XL)
    mixed = lax.dot_general(
        head_all.reshape(xl * chunk, head_cols),
        output_matrix,
        (((1,), (1,)), ((), ())),
        preferred_element_type=f32,
    ).astype(bf16)
    mixed = swap_blocks(mixed.reshape(xl * n_h, tokens, depth), XLH)
    mixed = jnp.sum(mixed.reshape(xl, n_h, tokens, depth).astype(f32), axis=1).astype(bf16)
    return mixed.transpose(1, 0, 2).reshape(1, tokens, width)


def solution(mesh):
    fine = Mesh(mesh.devices.reshape(4, 2, 2, 4, 4, 2), ("x", "l", "c", "h", "r", "q"))
    section, tensor = ("x", "l", "c"), ("h", "r", "q")
    by_row = P(section + tensor, None)
    return jax.shard_map(
        on_device,
        mesh=fine,
        in_specs=(P(section, tensor, None), P(), P(section)) + (by_row,) * 12,
        out_specs=P(section, tensor, None),
        check_vma=False,
    )
```
